128 devices in a mesh: det: 8 (over z, core), scan: 16 (over x, y).
Axes of the slice: x: 4, y: 4, z: 4, core: 2. Of those that a mesh axis runs over, the one named last changes fastest.
Arguments:
- intensity: bfloat16 [576, 512, 512], P('det', 'scan'), may hold values from -6 to 6
- aberrations: float32 [3], replicated, may hold values from 0.5 to 1.5
- lune_blocks: int32 [8, 16, 16], replicated, may hold values from 0 to 71, as said below
- lune_weight: int32 [8, 16, 16], replicated, may hold values from -1 to 1, as said below
Outputs:
- image: float32 [2, 512, 512], P(None, ('det', 'scan'))
The draws below stay inside these ranges and needn't reach their ends.
Inputs may be any that keep to these rules, and one draw needn't show every extreme that they name: `lune_blocks`: each tile's list holds 16 different detector blocks. Counting a tile's blocks by detector shard (block b lies in shard b // 9), exactly one shard holds 4 of them; of the other seven shards, five hold 2 and two hold 1. `lune_weight`: every entry is -1 or +1, never 0.
All inputs are finite; a program needn't handle non-finite values.
Results may differ from the reference program's by a relative error of at most 0.0052.
Values may be sent and summed in bfloat16 or wider, within the bound.
No kernel may reach another device: no remote copies, remote signals or barrier semaphores. Data moves between devices by JAX's collectives and lax.ppermute only.
A program may use at most 256 MiB of HBM per device.

```python
import math
import jax
import jax.numpy as jnp
from jax import lax

NS = 512
DSIDE = 24
BLK = 8
LMAX = 16
MOST = 4
NPIX = 576
NBLK = 72
BPD = 9
QT1 = 8
QT2 = 16
TQ1 = 64
TQ2 = 32
N_DET = 8


def shard_permutation(shard_key):
    return jax.random.permutation(shard_key, BPD).astype(jnp.int32)


def tile_list(tile_key):
    key_center, key_rank, key_blocks, key_order = jax.random.split(tile_key, 4)
    center = jax.random.randint(key_center, (), 0, N_DET).astype(jnp.int32)
    others = LMAX - MOST
    base_count = others // (N_DET - 1)
    extra_count = others % (N_DET - 1)
    ranking = jax.random.permutation(key_rank, N_DET - 1).astype(jnp.int32)
    other_rank = jnp.arange(N_DET - 1, dtype=jnp.int32)
    other_shards = other_rank + (other_rank >= center).astype(jnp.int32)
    counts = jnp.zeros((N_DET,), jnp.int32).at[other_shards].set(base_count + (ranking < extra_count).astype(jnp.int32))
    counts = counts.at[center].set(MOST)
    shard_keys = jax.random.split(key_blocks, N_DET)
    block_perms = jax.vmap(shard_permutation)(shard_keys)
    candidates = (jnp.arange(N_DET, dtype=jnp.int32)[:, None] * BPD + block_perms).reshape(-1)
    is_valid = (jnp.arange(BPD, dtype=jnp.int32)[None, :] < counts[:, None]).reshape(-1)
    position = jnp.arange(N_DET * BPD, dtype=jnp.int32)
    sort_key = jnp.where(is_valid, position, position + N_DET * BPD)
    picked = candidates[jnp.argsort(sort_key)[:LMAX]]
    return picked[jax.random.permutation(key_order, LMAX)]


def draw_lune_blocks(key, part):
    tile_keys = jax.random.split(jax.random.fold_in(key, 11), QT1 * QT2)
    return jax.vmap(tile_list)(tile_keys).reshape(QT1, QT2, LMAX).astype(jnp.int32)


def draw_lune_weight(key, part):
    side_key = jax.random.fold_in(key, 23)
    return (2 * jax.random.randint(side_key, (QT1, QT2, LMAX), 0, 2) - 1).astype(jnp.int32)


def shard_levels(key, dims, cuts, smallest, largest):
    gain, own = 1.0, jax.random.fold_in(key, 6)
    for dim, blocks in cuts:
        draws = jnp.exp(jax.random.uniform(jax.random.fold_in(own, dim), (blocks,), jnp.float32, smallest / len(cuts), largest / len(cuts)))
        gain = gain * jnp.repeat(draws, dims[dim] // blocks).reshape([-1 if axis == dim else 1 for axis in range(len(dims))])
    return gain


def noise(key, dims, deviation, reach, pieces=(), kind=jnp.bfloat16):
    entries = deviation * jax.random.normal(key, dims, jnp.float32)
    if pieces:
        entries = entries * shard_levels(key, dims, pieces, -0.22, 0.18)
    return jnp.clip(entries, -reach, reach).astype(kind)


def setup_inputs(seed: int = 0) -> dict:
    streams_of = jax.random.split(jax.random.key(seed), 5)
    intensity = noise(streams_of[0], (NPIX, NS, NS), 1.0, 6.0, ((0, 8), (1, 16)))
    aberrations = jnp.clip(jax.random.uniform(streams_of[1], (3,), jnp.float32, 0.5, 1.5), 0.5, 1.5)
    lune_blocks = draw_lune_blocks(jax.random.fold_in(streams_of[4], 71), 0)
    lune_weight = draw_lune_weight(jax.random.fold_in(streams_of[4], 71), 0)
    return {"intensity": intensity, "aberrations": aberrations, "lune_blocks": lune_blocks, "lune_weight": lune_weight}


freq_span = 4.0
detector_extent = 2.4
quartic_factor = 0.05

def dft_tables(length):
    counter = jnp.arange(length, dtype=jnp.int32)
    product = counter[:, None] * counter[None, :] % length
    angles = product.astype(jnp.float32) * (2.0 * math.pi / length)
    return (jnp.cos(angles), jnp.sin(angles))

def frequency(counter, length):
    shifted = (counter + length // 2) % length - length // 2
    return shifted.astype(jnp.float32) * (freq_span / length)

def detector_position(pixels):
    centre = (DSIDE - 1) / 2.0
    pitch_size = detector_extent / DSIDE
    pos_x = ((pixels % DSIDE).astype(jnp.float32) - centre) * pitch_size
    pos_y = ((pixels // DSIDE).astype(jnp.float32) - centre) * pitch_size
    return (pos_x, pos_y)

def aberration_phase(along_x, along_y, aberrations):
    radius = along_x * along_x + along_y * along_y
    return math.pi * (aberrations[0] * radius + quartic_factor * aberrations[1] * radius * radius + aberrations[2] * (along_x * along_x - along_y * along_y))

def lune_terms(spec_re, spec_im, weight_sign, pos_x, pos_y, freq_x, freq_y, aberrations):
    phase = aberration_phase(pos_x, pos_y, aberrations) - aberration_phase(pos_x - weight_sign * freq_x, pos_y - weight_sign * freq_y, aberrations)
    cos_phase = jnp.cos(phase)
    sin_phase = jnp.sin(phase)
    real_part = weight_sign * spec_re * cos_phase - spec_im * sin_phase
    imag_part = weight_sign * spec_im * cos_phase + spec_re * sin_phase
    return (real_part, imag_part)

def reference(intensity, aberrations, lune_blocks, lune_weight):
    maximum_level = lax.Precision.HIGHEST
    cosine_table, sine_table = dft_tables(NS)
    cos_low = cosine_table.astype(jnp.bfloat16)
    sin_low = sine_table.astype(jnp.bfloat16)
    table_row_count = jnp.stack([cos_low, -sin_low]).astype(jnp.float32)
    table_cols = jnp.stack([jnp.stack([cos_low, sin_low]), jnp.stack([-sin_low, cos_low])]).astype(jnp.float32)
    freq_all = frequency(jnp.arange(NS, dtype=jnp.int32), NS)
    block_ids = jnp.arange(NBLK, dtype=jnp.int32)
    matches = lune_blocks[..., None] == block_ids
    tile_lune_weight = lax.optimization_barrier(jnp.sum(jnp.where(matches, lune_weight[..., None], 0), axis=2)).astype(jnp.int32)

    def block_step(carry, block_id):
        block_payload = lax.dynamic_slice_in_dim(intensity, block_id * BLK, BLK, 0).astype(jnp.float32)
        row_fourier_spectrum = jnp.einsum('tlf,inf->tlin', block_payload, table_row_count, precision=maximum_level)
        row_fourier_spectrum = lax.optimization_barrier(row_fourier_spectrum.astype(jnp.bfloat16)).astype(jnp.float32)
        spectrum = jnp.einsum('oiqr,pric->pocq', table_cols, row_fourier_spectrum, precision=maximum_level)
        spectrum = lax.optimization_barrier((spectrum * (1.0 / NS)).astype(jnp.bfloat16)).astype(jnp.float32)
        weights = tile_lune_weight[:, :, block_id]
        weight_full = jnp.repeat(jnp.repeat(weights, TQ1, axis=0), TQ2, axis=1).astype(jnp.float32)
        weight_sign = weight_full.T[None]
        pixels = block_id * BLK + jnp.arange(BLK, dtype=jnp.int32)
        pos_x, pos_y = detector_position(pixels)
        real_part, imag_part = lune_terms(spectrum[:, 0], spectrum[:, 1], weight_sign, pos_x[:, None, None], pos_y[:, None, None], freq_all[None, :, None], freq_all[None, None, :], aberrations)
        carry = carry + jnp.stack([lax.optimization_barrier(jnp.sum(real_part, axis=0)), lax.optimization_barrier(jnp.sum(imag_part, axis=0))])
        return (carry, None)
    start_tile = jnp.zeros((2, NS, NS), jnp.float32)
    lune_sum, _ = lax.scan(block_step, start_tile, block_ids)
    lune_sum = lune_sum * (1.0 / math.sqrt(LMAX * BLK))
    psi_re = lune_sum[0].T
    psi_im = lune_sum[1].T
    back_re = jnp.dot(cosine_table, psi_re, precision=maximum_level) - jnp.dot(sine_table, psi_im, precision=maximum_level)
    back_im = jnp.dot(sine_table, psi_re, precision=maximum_level) + jnp.dot(cosine_table, psi_im, precision=maximum_level)
    image_re = (jnp.dot(back_re, cosine_table, precision=maximum_level) - jnp.dot(back_im, sine_table, precision=maximum_level)) * (1.0 / NS)
    image_im = (jnp.dot(back_re, sine_table, precision=maximum_level) + jnp.dot(back_im, cosine_table, precision=maximum_level)) * (1.0 / NS)
    return jnp.stack([image_re, image_im])
```

```python
import math

import jax
import jax.numpy as jnp
import numpy as np
from jax import lax
from jax.experimental import pallas as pl
from jax.experimental.pallas import tpu as pltpu
from jax.sharding import PartitionSpec as P

DSIDE = 24
BLK = 8
N = 512
DET = 8
SCAN = 16
BPD = 9
COLS = 16
ROWS = N // SCAN
TILE_ROWS = N // DET
FREQ_STEP = 4.0 / N
PITCH = 2.4 / DSIDE
CENTRE = (DSIDE - 1) / 2.0
QUARTIC = 0.05
SCALE = 1.0 / (N * N * math.sqrt(16 * BLK))


def poly_tables():
    nodes = (0.5 * np.cos((np.arange(64) + 0.5) * np.pi / 64)) ** 2
    z = np.concatenate([nodes, [0.0]])
    x = np.sqrt(z)
    cos_c = np.polynomial.polynomial.polyfit(z, np.cos(2 * np.pi * x), 6)
    ratio = 2 * np.pi * np.sinc(2 * x)
    sin_c = np.polynomial.polynomial.polyfit(z, ratio, 6)
    return [float(v) for v in cos_c], [float(v) for v in sin_c]


COS_C, SIN_C = poly_tables()


def dft_tables():
    n = np.arange(N)
    angle = (n[:, None] * n[None, :] % N) * (2.0 * np.pi / N)
    return np.cos(angle), np.sin(angle)


def constants():
    cos, sin = dft_tables()
    bf16 = jnp.bfloat16
    re_part = cos[:, : N // 2]
    im_part = -sin[:, : N // 2]
    im_part[:, 0] = cos[:, N // 2]
    row_table = np.concatenate([re_part, im_part], axis=1).astype(bf16)
    col_table = np.concatenate([cos, sin], axis=0).astype(bf16)
    c = np.arange(N // 2).reshape(SCAN, COLS)
    mirrored = N - c
    mirrored[0, 0] = N // 2
    order = np.stack([c, mirrored], axis=1).reshape(-1)
    last_table = np.concatenate([cos[order], sin[order]], axis=1).astype(bf16)
    return row_table, col_table, last_table


def row_kernel(x_ref, table_ref, o_ref):
    x = x_ref[...].reshape(BLK * ROWS, N)
    y = jnp.dot(x, table_ref[...], preferred_element_type=jnp.float32)
    group = lax.broadcasted_iota(jnp.int32, (ROWS, 128), 1) // COLS
    for part in range(2):
        for half in range(2):
            col = (part * 2 + half) * 128
            a = [y[ROWS * p : ROWS * (p + 1), col : col + 128] for p in range(BLK)]
            for k in range(3):
                width = COLS << k
                low = (group >> k) & 1 == 0
                for p in range(BLK):
                    if p >> k & 1:
                        continue
                    q = p | 1 << k
                    first = jnp.where(low, a[p], pltpu.roll(a[q], width, 1))
                    second = jnp.where(low, pltpu.roll(a[p], 128 - width, 1), a[q])
                    a[p], a[q] = first, second
            for d in range(BLK):
                o_ref[half * 8 + d, :, part * 128 : (part + 1) * 128] = a[d].astype(jnp.bfloat16)


def column_kernel(meta_ref, flags_ref, ab_ref, r_ref, table_ref, o_ref, pq_ref, acc_ref):
    b = pl.program_id(0)
    f32 = jnp.float32

    @pl.when(b == 0)
    def _():
        acc_ref[...] = jnp.zeros_like(acc_ref)

    pq_ref[...] = jnp.dot(table_ref[...], r_ref[...], preferred_element_type=f32)

    det = meta_ref[0]
    scan = meta_ref[1]
    a0, a1, a2 = ab_ref[0], ab_ref[1], ab_ref[2]
    kappa = QUARTIC * a1
    plus = a0 + a2
    minus = a0 - a2
    block = det * BPD + b
    lane = lax.broadcasted_iota(jnp.int32, (1, 128), 1)
    pix = lane // COLS
    col = lane % COLS
    column = scan * COLS + col
    special = column == 0
    keep = jnp.where(special, 0.0, 1.0)
    kx = ((lax.rem(block, 3) * BLK + pix).astype(f32) - CENTRE) * PITCH
    ky = (jnp.full((1, 128), lax.div(block, 3), jnp.int32).astype(f32) - CENTRE) * PITCH
    kx2 = kx * kx
    ky2 = ky * ky
    chi_k = plus * kx2 + minus * ky2 + kappa * (kx2 + ky2) * (kx2 + ky2)
    freq_direct = column.astype(f32) * FREQ_STEP
    freq_mirror = jnp.where(special, -(N // 2) * FREQ_STEP, -freq_direct)
    row = lax.broadcasted_iota(jnp.int32, (TILE_ROWS, 128), 0).astype(f32)

    def tile(t, _):
        start = pl.multiple_of(t * TILE_ROWS, TILE_ROWS)
        w_direct = flags_ref[b * 8 + t]
        w_mirror = flags_ref[72 + b * 8 + t]
        w_extra = flags_ref[144 + b * 8 + t]
        base = jnp.full((1, 128), start - jnp.where(t >= 4, N, 0), jnp.int32).astype(f32) * FREQ_STEP

        def add(w, freq_x, mirror):
            ux = kx - w * freq_x
            x2 = ux * ux
            fx = 0.5 * (chi_k - plus * x2 - kappa * x2 * x2)
            dx = -0.5 * minus - kappa * x2
            bx = -0.5 * kappa
            alpha = ky - w * base
            beta = -w * FREQ_STEP
            uy = alpha + beta * row
            y2 = uy * uy
            turns = fx + y2 * (dx + bx * y2)
            x = turns - jnp.floor(turns + 0.5)
            z = x * x
            cos = COS_C[6]
            for v in COS_C[5::-1]:
                cos = cos * z + v
            sin = SIN_C[6]
            for v in SIN_C[5::-1]:
                sin = sin * z + v
            if mirror:
                x = x * (w * w)
            sin = sin * x
            cos = cos * w
            p1 = pq_ref[pl.ds(start, TILE_ROWS), :128]
            p3 = pq_ref[pl.ds(start, TILE_ROWS), 128:]
            p2 = pq_ref[pl.ds(N + start, TILE_ROWS), :128]
            p4 = pq_ref[pl.ds(N + start, TILE_ROWS), 128:]
            if mirror:
                g_re = jnp.where(special, p3, p1 - p4)
                h_im = jnp.where(special, p4, p3 + p2)
                real = g_re * cos + h_im * sin
                imag = g_re * sin - h_im * cos
            else:
                g_re = p1 + keep * p4
                g_im = keep * p3 - p2
                real = g_re * cos - g_im * sin
                imag = g_re * sin + g_im * cos
            k = 1 if mirror else 0
            acc_ref[pl.ds(start, TILE_ROWS), k * 128 : (k + 1) * 128] += real
            acc_ref[pl.ds(start, TILE_ROWS), (k + 2) * 128 : (k + 3) * 128] += imag

        @pl.when(w_direct != 0)
        def _():
            add(jnp.full((1, 128), w_direct, jnp.int32).astype(f32), freq_direct, False)

        @pl.when(jnp.logical_or(w_mirror != 0, w_extra != 0))
        def _():
            w = jnp.where(col == 0, w_extra, w_mirror).astype(f32)
            add(w, freq_mirror, True)

        return 0

    lax.fori_loop(0, DET, tile, 0)

    @pl.when(b == BPD - 1)
    def _():
        src = lax.broadcasted_iota(jnp.int32, (N, 128), 0)
        dst = lax.broadcasted_iota(jnp.int32, (N, 128), 1)
        pick = (src // 128 == dst % 64 // COLS) & (src % COLS == dst % COLS)
        pick = jnp.where(pick, 1.0, 0.0).astype(jnp.bfloat16)
        lune = jnp.dot(acc_ref[...].astype(jnp.bfloat16), pick, preferred_element_type=f32)
        high = lune.astype(jnp.bfloat16).astype(f32)
        packed = jnp.where(dst < 64, high, lune - high).astype(jnp.bfloat16)
        g = jnp.dot(table_ref[...], packed, preferred_element_type=f32)
        g_cos = g[:N]
        g_sin = g[N:]
        is_re = dst // 32 % 2 == 0
        swapped = jnp.where(is_re, -pltpu.roll(g_sin, 96, 1), pltpu.roll(g_sin, 32, 1))
        out = g_cos + swapped
        out = out + pltpu.roll(out, 64, 1)
        o_ref[...] = out[:, :64].astype(jnp.bfloat16)


def last_kernel(y_ref, table_ref, o_ref):
    f32 = jnp.float32
    y = y_ref[0:64, :].astype(f32)
    for d in range(1, DET):
        y = y + y_ref[64 * d : 64 * (d + 1), :].astype(f32)
    top = lax.broadcasted_iota(jnp.int32, (8, 64), 0) < 4
    parts = []
    for half in range(2):
        pieces = []
        for u in range(8):
            rows = y[8 * u : 8 * (u + 1), :]
            pieces.append(jnp.where(top, rows, 0.0)[:, 32 * half : 32 * (half + 1)])
            pieces.append(jnp.where(top, 0.0, rows)[:, 32 * half : 32 * (half + 1)])
        parts.append(jnp.concatenate(pieces, axis=1))
    lhs = jnp.concatenate(parts, axis=0)
    high = lhs.astype(jnp.bfloat16)
    low = (lhs - high.astype(f32)).astype(jnp.bfloat16)
    out = jnp.dot(high, table_ref[...], preferred_element_type=f32)
    out = out + jnp.dot(low, table_ref[...], preferred_element_type=f32)
    re, im = out[0:8], out[8:16]
    image_re = re[:, :N] - im[:, N:]
    image_im = re[:, N:] + im[:, :N]
    o_ref[0] = (image_re[0:4] + image_re[4:8]) * SCALE
    o_ref[1] = (image_im[0:4] + image_im[4:8]) * SCALE


def shards(intensity, aberrations, lune_blocks, lune_weight):
    det = lax.axis_index("det").astype(jnp.int32)
    scan = lax.axis_index("scan").astype(jnp.int32)
    row_table, col_table, last_table = (jnp.asarray(v) for v in constants())
    bf16 = jnp.bfloat16

    half = scan // 2
    extra = jnp.where(scan % 2 == 0, jnp.where(scan == 0, 8, 16 - half), 15 - half)
    columns = jnp.stack([half, 15 - half, extra])
    blocks = jnp.take(lune_blocks, columns, axis=1)
    weights = jnp.take(lune_weight, columns, axis=1)
    own = det * BPD + jnp.arange(BPD, dtype=jnp.int32)
    hits = blocks[..., None] == own
    flags = jnp.sum(jnp.where(hits, weights[..., None], 0), axis=2)
    flags = flags.transpose(1, 2, 0).reshape(-1)
    meta = jnp.stack([det, scan])

    rows = pl.pallas_call(
        row_kernel,
        grid=(BPD,),
        in_specs=[
            pl.BlockSpec((BLK, ROWS, N), lambda b: (b, 0, 0)),
            pl.BlockSpec((N, N), lambda b: (0, 0)),
        ],
        out_specs=pl.BlockSpec((SCAN, ROWS, 256), lambda b: (0, 0, b)),
        out_shape=jax.ShapeDtypeStruct((SCAN, ROWS, BPD * 256), bf16),
        name="rows",
    )(intensity, row_table)

    spread = lax.all_to_all(rows.reshape(N, BPD * 256), "scan", 0, 0, tiled=True)

    smem = pl.BlockSpec(memory_space=pltpu.SMEM)
    back = pl.pallas_call(
        column_kernel,
        grid=(BPD,),
        in_specs=[
            smem,
            smem,
            smem,
            pl.BlockSpec((N, 256), lambda b: (0, b)),
            pl.BlockSpec((2 * N, N), lambda b: (0, 0)),
        ],
        out_specs=pl.BlockSpec((N, 64), lambda b: (0, 0)),
        out_shape=jax.ShapeDtypeStruct((N, 64), bf16),
        scratch_shapes=[
            pltpu.VMEM((2 * N, 256), jnp.float32),
            pltpu.VMEM((N, 512), jnp.float32),
        ],
        name="columns",
    )(meta, flags, aberrations, spread, col_table)

    parts = lax.all_to_all(back, ("det", "scan"), 0, 0, tiled=True)

    return pl.pallas_call(
        last_kernel,
        out_shape=jax.ShapeDtypeStruct((2, 4, N), jnp.float32),
        name="last",
    )(parts, last_table)


def solution(mesh):
    return jax.shard_map(
        shards,
        mesh=mesh,
        in_specs=(P("det", "scan", None), P(), P(), P()),
        out_specs=P(None, ("det", "scan"), None),
        check_vma=False,
    )
```

```python
import math

import jax
import jax.numpy as jnp
import numpy as np
from jax import lax
from jax.experimental import pallas as pl
from jax.experimental.pallas import tpu as pltpu
from jax.sharding import PartitionSpec as P

DSIDE = 24
BLK = 8
N = 512
DET = 8
SCAN = 16
BPD = 9
GROUP = 3
COLS = 16
ROWS = N // SCAN
TILE_ROWS = N // DET
FREQ_STEP = 4.0 / N
PITCH = 2.4 / DSIDE
CENTRE = (DSIDE - 1) / 2.0
QUARTIC = 0.05
SCALE = 1.0 / (N * N * math.sqrt(16 * BLK))


def poly_tables():
    nodes = (0.5 * np.cos((np.arange(64) + 0.5) * np.pi / 64)) ** 2
    z = np.concatenate([nodes, [0.0]])
    x = np.sqrt(z)
    cos_c = np.polynomial.polynomial.polyfit(z, np.cos(2 * np.pi * x), 6)
    ratio = 2 * np.pi * np.sinc(2 * x)
    sin_c = np.polynomial.polynomial.polyfit(z, ratio, 6)
    return [float(v) for v in cos_c], [float(v) for v in sin_c]


COS_C, SIN_C = poly_tables()


def dft_tables():
    n = np.arange(N)
    angle = (n[:, None] * n[None, :] % N) * (2.0 * np.pi / N)
    return np.cos(angle), np.sin(angle)


def constants():
    cos, sin = dft_tables()
    bf16 = jnp.bfloat16
    re_part = cos[:, : N // 2]
    im_part = -sin[:, : N // 2]
    im_part[:, 0] = cos[:, N // 2]
    row_table = np.concatenate([re_part, im_part], axis=1).astype(bf16)
    col_table = np.concatenate([cos, sin], axis=0).astype(bf16)
    c = np.arange(N // 2).reshape(SCAN, COLS)
    mirrored = N - c
    mirrored[0, 0] = N // 2
    order = np.stack([c, mirrored], axis=1).reshape(-1)
    last_table = np.concatenate([cos[order], sin[order]], axis=1).astype(bf16)
    return row_table, col_table, last_table


def row_kernel(x_hbm, table_hbm, o_hbm, x_ref, table_ref, o_ref, sems, out_sems):
    copies = [pltpu.make_async_copy(table_hbm, table_ref, sems.at[BPD])]
    for b in range(BPD):
        here = pl.ds(b * BLK, BLK)
        copies.append(pltpu.make_async_copy(x_hbm.at[here], x_ref.at[here], sems.at[b]))
    for copy in copies:
        copy.start()
    copies[0].wait()
    group = lax.broadcasted_iota(jnp.int32, (ROWS, 128), 1) // COLS
    bits = [(group >> k) & 1 == 1 for k in range(3)]
    for b in range(BPD):
        copies[1 + b].wait()
        x = x_ref[b * BLK : (b + 1) * BLK].reshape(BLK * ROWS, N)
        for part in range(2):
            y = jnp.dot(x, table_ref[:, part * 256 : (part + 1) * 256], preferred_element_type=jnp.float32)
            y = y.astype(jnp.bfloat16)
            for half in range(2):
                a = [y[ROWS * p : ROWS * (p + 1), half * 128 : (half + 1) * 128] for p in range(BLK)]
                for k in range(3):
                    a = [jnp.where(bits[k], a[(p + (1 << k)) % BLK], a[p]) for p in range(BLK)]
                a = [a[0]] + [pltpu.roll(a[p], COLS * p, 1) for p in range(1, BLK)]
                for k in range(3):
                    a = [jnp.where(bits[k], a[(p + (1 << k)) % BLK], a[p]) for p in range(BLK)]
                col = (b * 2 + part) * 128
                for d in range(BLK):
                    o_ref[half * 8 + d, :, col : col + 128] = a[-d % BLK]
        here = pl.ds(b * 256, 256)
        copies.append(pltpu.make_async_copy(o_ref.at[:, :, here], o_hbm.at[:, :, here], out_sems.at[b]))
        copies[-1].start()
    for copy in copies[BPD + 1 :]:
        copy.wait()


def phase_kernel(meta_ref, flags_ref, ab_ref, o_ref, pick_ref):
    f32 = jnp.float32
    b = pl.program_id(0)

    @pl.when(b == 0)
    def _():
        src = lax.broadcasted_iota(jnp.int32, (N, 256), 0)
        dst = lax.broadcasted_iota(jnp.int32, (N, 256), 1)
        for_sin = dst >= 128
        same = (src // 128 % 2 == dst // COLS % 2) & (src % COLS == dst % COLS)
        src_im = src // 256
        dst_im = dst // 32 % 2
        sign = jnp.where(for_sin & (dst_im == 0), -1.0, 1.0)
        match = (src_im == dst_im) != for_sin
        pick_ref[...] = jnp.where(same & match, sign, 0.0).astype(jnp.bfloat16)

    det = meta_ref[0]
    scan = meta_ref[1]
    a0, a1, a2 = ab_ref[0], ab_ref[1], ab_ref[2]
    kappa = QUARTIC * a1
    plus = a0 + a2
    minus = a0 - a2
    lane = lax.broadcasted_iota(jnp.int32, (1, 128), 1)
    pix = lane // COLS
    col = lane % COLS
    column = scan * COLS + col
    special = column == 0
    freq_direct = column.astype(f32) * FREQ_STEP
    freq_mirror = jnp.where(special, -(N // 2) * FREQ_STEP, -freq_direct)
    row = lax.broadcasted_iota(jnp.int32, (TILE_ROWS, 128), 0).astype(f32)

    def tile(t, _):
        i = b * DET + t
        start = pl.multiple_of(t * TILE_ROWS, TILE_ROWS)
        block = det * BPD + b
        kx = ((lax.rem(block, 3) * BLK + pix).astype(f32) - CENTRE) * PITCH
        ky = (jnp.full((1, 128), lax.div(block, 3), jnp.int32).astype(f32) - CENTRE) * PITCH
        kx2 = kx * kx
        ky2 = ky * ky
        chi_k = plus * kx2 + minus * ky2 + kappa * (kx2 + ky2) * (kx2 + ky2)
        w_direct = flags_ref[i]
        w_mirror = flags_ref[72 + i]
        w_extra = flags_ref[144 + i]
        base = jnp.full((1, 128), start - jnp.where(t >= 4, N, 0), jnp.int32).astype(f32) * FREQ_STEP

        def put(k, any_entry, w, freq_x):
            @pl.when(any_entry)
            def _():
                ux = kx - w * freq_x
                x2 = ux * ux
                fx = 0.5 * (chi_k - plus * x2 - kappa * x2 * x2)
                dx = -0.5 * minus - kappa * x2
                bx = -0.5 * kappa
                uy = (ky - w * base) - (w * FREQ_STEP) * row
                y2 = uy * uy
                turns = fx + y2 * (dx + bx * y2)
                x = turns - jnp.floor(turns + 0.5)
                z = x * x
                cos = COS_C[6]
                for v in COS_C[5::-1]:
                    cos = cos * z + v
                sin = SIN_C[6]
                for v in SIN_C[5::-1]:
                    sin = sin * z + v
                o_ref[0, pl.ds(start, TILE_ROWS), k * 128 : (k + 1) * 128] = cos * w
                o_ref[0, pl.ds(start, TILE_ROWS), (k + 1) * 128 : (k + 2) * 128] = sin * (x * (w * w))

            @pl.when(jnp.logical_not(any_entry))
            def _():
                o_ref[0, pl.ds(start, TILE_ROWS), k * 128 : (k + 2) * 128] = jnp.zeros((TILE_ROWS, 256), f32)

        put(0, w_direct != 0, jnp.full((1, 128), w_direct, jnp.int32).astype(f32), freq_direct)
        w = jnp.where(col == 0, w_extra, w_mirror).astype(f32)
        put(2, jnp.logical_or(w_mirror != 0, w_extra != 0), w, freq_mirror)
        return 0

    lax.fori_loop(0, DET, tile, 0)


def column_kernel(meta_ref, r_ref, phase_hbm, pick_hbm, table_ref, o_ref, *scratch):
    pq_ref, acc_ref, out_ref, phase_ref, pick_ref, sems = scratch
    f32 = jnp.float32
    bf16 = jnp.bfloat16
    copies = [pltpu.make_async_copy(phase_hbm.at[b], phase_ref.at[b], sems.at[b]) for b in range(BPD)]
    copies.append(pltpu.make_async_copy(pick_hbm, pick_ref, sems.at[BPD]))
    for copy in copies:
        copy.start()
    lane = lax.broadcasted_iota(jnp.int32, (1, 128), 1)
    special = meta_ref[1] * COLS + lane % COLS == 0
    keep = jnp.where(special, 0.0, 1.0)
    size = GROUP * 256
    step = 32

    def products(g):
        pq_ref[g % 2] = jnp.dot(table_ref[...], r_ref[:, g * size : (g + 1) * size], preferred_element_type=f32)

    def lunes(g):
        for i in range(GROUP):
            copies[g * GROUP + i].wait()
        for q in range(0, N, step):
            sums = [0.0] * 4 if g == 0 else [acc_ref[q : q + step, k * 128 : (k + 1) * 128] for k in range(4)]
            for i in range(GROUP):
                here = slice(i * 256, i * 256 + 128)
                there = slice(i * 256 + 128, i * 256 + 256)
                p1 = pq_ref[g % 2, q : q + step, here]
                p3 = pq_ref[g % 2, q : q + step, there]
                p2 = pq_ref[g % 2, N + q : N + q + step, here]
                p4 = pq_ref[g % 2, N + q : N + q + step, there]
                cos, sin, cos_m, sin_m = [
                    phase_ref[g * GROUP + i, q : q + step, k * 128 : (k + 1) * 128] for k in range(4)
                ]
                g_re = p1 + keep * p4
                g_im = keep * p3 - p2
                m_re = jnp.where(special, p3, p1 - p4)
                m_im = jnp.where(special, p4, p3 + p2)
                sums[0] += g_re * cos - g_im * sin
                sums[1] += m_re * cos_m + m_im * sin_m
                sums[2] += g_re * sin + g_im * cos
                sums[3] += m_re * sin_m - m_im * cos_m
            for k in range(4):
                acc_ref[q : q + step, k * 128 : (k + 1) * 128] = sums[k]

    products(0)
    for g in range(1, BPD // GROUP):
        products(g)
        lunes(g - 1)
    lunes(BPD // GROUP - 1)

    copies[BPD].wait()
    lune = jnp.dot(acc_ref[...].astype(bf16), pick_ref[...], preferred_element_type=f32)
    high = lune.astype(bf16).astype(f32)
    is_high = lax.broadcasted_iota(jnp.int32, (N, 256), 1) % 128 < 64
    packed = jnp.where(is_high, high, lune - high).astype(bf16)
    out_ref[...] = jnp.dot(table_ref[:N], packed[:, :128], preferred_element_type=f32) + jnp.dot(
        table_ref[N:], packed[:, 128:], preferred_element_type=f32
    )
    even = out_ref[pl.ds(0, N // 2, stride=2), :]
    odd = out_ref[pl.ds(1, N // 2, stride=2), :]
    first = lane < 64
    out = jnp.where(first, even, odd) + pltpu.roll(jnp.where(first, odd, even), 64, 1)
    o_ref[...] = out.astype(bf16)


def last_kernel(y_ref, table_ref, o_ref):
    f32 = jnp.float32
    bf16 = jnp.bfloat16
    y = y_ref[0:32, :].astype(f32)
    for d in range(1, DET):
        y = y + y_ref[32 * d : 32 * (d + 1), :].astype(f32)
    group = lax.broadcasted_iota(jnp.int32, (8, 128), 1) // 32
    own = lax.broadcasted_iota(jnp.int32, (8, 128), 0) // 2
    tiles = [[] for _ in range(4)]
    for u in range(4):
        rows = y[8 * u : 8 * (u + 1), :]
        turned = [rows] + [pltpu.roll(rows, 32 * k, 1) for k in range(1, 4)]
        for q in range(4):
            tile = jnp.zeros((8, 128), f32)
            for v in range(4):
                tile = jnp.where((own == v) & (group == v), turned[(v - q) % 4], tile)
            tiles[q].append(tile)
    lhs = jnp.concatenate([jnp.concatenate(tiles[q], axis=1) for q in range(4)], axis=0)
    high = lhs.astype(bf16)
    low = (lhs - high.astype(f32)).astype(bf16)
    both = jnp.concatenate([high, low], axis=0)
    out = jnp.dot(both, table_ref[...], preferred_element_type=f32)
    out = out[:32] + out[32:]
    for par in range(2):
        re = out[16 * par : 16 * par + 8]
        im = out[16 * par + 8 : 16 * par + 16]
        image_re = re[:, :N] - im[:, N:]
        image_im = re[:, N:] + im[:, :N]
        for k, image in enumerate((image_re, image_im)):
            image = image[0:4] + image[4:8]
            image = (image[0:2] + image[2:4]) * SCALE
            for h in range(2):
                o_ref[k, 2 * h + par : 2 * h + par + 1, :] = image[h : h + 1]


def shards(intensity, aberrations, lune_blocks, lune_weight):
    det = lax.axis_index("det").astype(jnp.int32)
    scan = lax.axis_index("scan").astype(jnp.int32)
    row_table, col_table, last_table = (jnp.asarray(v) for v in constants())
    bf16 = jnp.bfloat16
    f32 = jnp.float32

    half = scan // 2
    extra = jnp.where(scan % 2 == 0, jnp.where(scan == 0, 8, 16 - half), 15 - half)
    columns = jnp.stack([half, 15 - half, extra])
    blocks = jnp.take(lune_blocks, columns, axis=1)
    weights = jnp.take(lune_weight, columns, axis=1)
    own = det * BPD + jnp.arange(BPD, dtype=jnp.int32)
    hits = blocks[..., None] == own
    flags = jnp.sum(jnp.where(hits, weights[..., None], 0), axis=2)
    flags = flags.transpose(1, 2, 0).reshape(-1)
    meta = jnp.stack([det, scan])

    smem = pl.BlockSpec(memory_space=pltpu.SMEM)
    vmem = pl.BlockSpec(memory_space=pltpu.VMEM)
    hbm = pl.BlockSpec(memory_space=pl.ANY)

    def in_hbm(v):
        return pltpu.with_memory_space_constraint(v, pltpu.HBM)

    def on_chip(v):
        return pltpu.with_memory_space_constraint(v, pltpu.VMEM)

    rows = pl.pallas_call(
        row_kernel,
        in_specs=[hbm, hbm],
        out_specs=hbm,
        out_shape=pltpu.HBM((SCAN, ROWS, BPD * 256), bf16),
        scratch_shapes=[
            pltpu.VMEM((BPD * BLK, ROWS, N), bf16),
            pltpu.VMEM((N, N), bf16),
            pltpu.VMEM((SCAN, ROWS, BPD * 256), bf16),
            pltpu.SemaphoreType.DMA((BPD + 1,)),
            pltpu.SemaphoreType.DMA((BPD,)),
        ],
        compiler_params=pltpu.CompilerParams(vmem_limit_bytes=10 << 20),
        name="rows",
    )(in_hbm(intensity), in_hbm(row_table))

    spread = lax.all_to_all(rows.reshape(N, BPD * 256), "scan", 0, 0, tiled=True)

    phases, pick = pl.pallas_call(
        phase_kernel,
        grid=(BPD,),
        in_specs=[smem, smem, smem],
        out_specs=[pl.BlockSpec((1, N, N), lambda b: (b, 0, 0)), pl.BlockSpec((N, 256), lambda b: (0, 0))],
        out_shape=[pltpu.HBM((BPD, N, N), f32), pltpu.HBM((N, 256), bf16)],
        compiler_params=pltpu.CompilerParams(vmem_limit_bytes=8 << 20),
        name="phases",
    )(meta, flags, aberrations)

    back = pl.pallas_call(
        column_kernel,
        in_specs=[smem, vmem, hbm, hbm, vmem],
        out_specs=vmem,
        out_shape=jax.ShapeDtypeStruct((N // 2, 128), bf16),
        scratch_shapes=[
            pltpu.VMEM((2, 2 * N, GROUP * 256), f32),
            pltpu.VMEM((N, N), f32),
            pltpu.VMEM((N, 128), f32),
            pltpu.VMEM((BPD, N, N), f32),
            pltpu.VMEM((N, 256), bf16),
            pltpu.SemaphoreType.DMA((BPD + 1,)),
        ],
        compiler_params=pltpu.CompilerParams(vmem_limit_bytes=36 << 20),
        name="columns",
    )(meta, on_chip(spread), in_hbm(phases), in_hbm(pick), on_chip(col_table))

    parts = lax.all_to_all(back.reshape(DET * SCAN, 2, 128), ("det", "scan"), 0, 0, tiled=True)

    return pl.pallas_call(
        last_kernel,
        in_specs=[vmem, vmem],
        out_specs=vmem,
        out_shape=jax.ShapeDtypeStruct((2, 4, N), f32),
        compiler_params=pltpu.CompilerParams(vmem_limit_bytes=6 << 20),
        name="last",
    )(parts.reshape(N // 2, 128), on_chip(last_table))


def solution(mesh):
    return jax.shard_map(
        shards,
        mesh=mesh,
        in_specs=(P("det", "scan", None), P(), P(), P()),
        out_specs=P(None, ("det", "scan"), None),
        check_vma=False,
    )
```

```python
import math

import jax
import jax.numpy as jnp
import numpy as np
from jax import lax
from jax.experimental import pallas as pl
from jax.experimental.pallas import tpu as pltpu
from jax.sharding import PartitionSpec as P

DSIDE = 24
BLK = 8
N = 512
DET = 8
SCAN = 16
BPD = 9
HALF = N // 2
LEFT = HALF + 8
GROUP = 3
STEP = 16
WAITS = {0: (1, 2), 2: (3, 4, 5, 6, 7, 8)}
SENDS = (2, 5, 7, 8)
PIECE = 64
COLS = 16
ROWS = N // SCAN
TILE_ROWS = N // DET
FREQ_STEP = 4.0 / N
PITCH = 2.4 / DSIDE
CENTRE = (DSIDE - 1) / 2.0
QUARTIC = 0.05
SCALE = 1.0 / (N * N * math.sqrt(16 * BLK))


def poly_tables():
    nodes = (0.5 * np.cos((np.arange(64) + 0.5) * np.pi / 64)) ** 2
    z = np.concatenate([nodes, [0.0]])
    x = np.sqrt(z)
    cos_c = np.polynomial.polynomial.polyfit(z, np.cos(2 * np.pi * x), 6)
    ratio = 2 * np.pi * np.sinc(2 * x)
    sin_c = np.polynomial.polynomial.polyfit(z, ratio, 6)
    return [float(v) for v in cos_c], [float(v) for v in sin_c]


COS_C, SIN_C = poly_tables()


def dft_tables():
    n = np.arange(N)
    angle = (n[:, None] * n[None, :] % N) * (2.0 * np.pi / N)
    return np.cos(angle), np.sin(angle)


def constants():
    cos, sin = dft_tables()
    bf16 = jnp.bfloat16
    re_part = cos[:, : N // 2]
    im_part = -sin[:, : N // 2]
    im_part[:, 0] = cos[:, N // 2]
    row_table = np.concatenate([re_part, im_part], axis=1).astype(bf16)
    col_table = np.concatenate([sin[HALF:], sin[:HALF], cos], axis=0).astype(bf16)
    c = np.arange(N // 2).reshape(SCAN, COLS)
    mirrored = N - c
    mirrored[0, 0] = N // 2
    order = np.stack([c, mirrored], axis=1).reshape(-1)
    last_table = np.concatenate([cos[order], sin[order]], axis=1).astype(bf16)
    return row_table, col_table, last_table


def row_kernel(x_hbm, table_hbm, o_hbm, x_ref, table_ref, y_ref, o_ref, sems, out_sems):
    copies = [pltpu.make_async_copy(table_hbm, table_ref, sems.at[BPD])]
    for b in range(BPD):
        here = pl.ds(b * BLK, BLK)
        copies.append(pltpu.make_async_copy(x_hbm.at[here], x_ref.at[here], sems.at[b]))
    for copy in copies:
        copy.start()
    group = lax.broadcasted_iota(jnp.int32, (ROWS, 128), 1) // COLS
    bits = [(group >> k) & 1 == 1 for k in range(3)]

    def transform(b):
        x = x_ref[b * BLK : (b + 1) * BLK].reshape(BLK * ROWS, N)
        y_ref[...] = jnp.dot(x, table_ref[...], preferred_element_type=jnp.float32)

    def exchange(b):
        for part in range(2):
            for half in range(2):
                col = (part * 2 + half) * 128
                a = [y_ref[ROWS * p : ROWS * (p + 1), col : col + 128].astype(jnp.bfloat16) for p in range(BLK)]
                for k in range(3):
                    a = [jnp.where(bits[k], a[(p + (1 << k)) % BLK], a[p]) for p in range(BLK)]
                a = [a[0]] + [pltpu.roll(a[p], COLS * p, 1) for p in range(1, BLK)]
                for k in range(3):
                    a = [jnp.where(bits[k], a[(p + (1 << k)) % BLK], a[p]) for p in range(BLK)]
                col = (b * 2 + part) * 128
                for d in range(BLK):
                    o_ref[half * 8 + d, :, col : col + 128] = a[-d % BLK]

    outs = []
    sent = 0
    copies[0].wait()
    copies[1].wait()
    transform(0)
    for b in range(BPD):
        for i in WAITS.get(b, ()):
            copies[1 + i].wait()
        exchange(b)
        if b + 1 < BPD:
            transform(b + 1)
        if b in SENDS:
            here = pl.ds(sent * 256, (b + 1 - sent) * 256)
            outs.append(pltpu.make_async_copy(o_ref.at[:, :, here], o_hbm.at[:, :, here], out_sems.at[len(outs)]))
            outs[-1].start()
            sent = b + 1
    for copy in outs:
        copy.wait()


def phase_kernel(meta_ref, flags_ref, ab_ref, o_ref, pick_ref):
    f32 = jnp.float32
    b = pl.program_id(0)

    @pl.when(b == 0)
    def _():
        src = lax.broadcasted_iota(jnp.int32, (N, 256), 0)
        dst = lax.broadcasted_iota(jnp.int32, (N, 256), 1)
        for_sin = dst >= 128
        same = (src // 128 % 2 == dst // COLS % 2) & (src % COLS == dst % COLS)
        src_im = src // 256
        dst_im = dst // 32 % 2
        sign = jnp.where(for_sin & (dst_im == 0), -1.0, 1.0)
        match = (src_im == dst_im) != for_sin
        pick_ref[...] = jnp.where(same & match, sign, 0.0).astype(jnp.bfloat16)

    det = meta_ref[0]
    scan = meta_ref[1]
    a0, a1, a2 = ab_ref[0], ab_ref[1], ab_ref[2]
    kappa = QUARTIC * a1
    plus = a0 + a2
    minus = a0 - a2
    lane = lax.broadcasted_iota(jnp.int32, (1, 128), 1)
    pix = lane // COLS
    col = lane % COLS
    column = scan * COLS + col
    special = column == 0
    freq_direct = column.astype(f32) * FREQ_STEP
    freq_mirror = jnp.where(special, -(N // 2) * FREQ_STEP, -freq_direct)
    row = lax.broadcasted_iota(jnp.int32, (TILE_ROWS, 128), 0)
    block = det * BPD + b
    kx = ((lax.rem(block, 3) * BLK + pix).astype(f32) - CENTRE) * PITCH
    ky = (jnp.full((1, 128), lax.div(block, 3), jnp.int32).astype(f32) - CENTRE) * PITCH
    kx2 = kx * kx
    ky2 = ky * ky
    chi_k = plus * kx2 + minus * ky2 + kappa * (kx2 + ky2) * (kx2 + ky2)

    def put(k, start, any_entry, w, freq_x, freq_y):
        here = pl.ds(start, TILE_ROWS)

        @pl.when(any_entry)
        def _():
            ux = kx - w * freq_x
            x2 = ux * ux
            fx = 0.5 * (chi_k - plus * x2 - kappa * x2 * x2)
            dx = -0.5 * minus - kappa * x2
            bx = -0.5 * kappa
            uy = ky - w * freq_y
            y2 = uy * uy
            turns = fx + y2 * (dx + bx * y2)
            x = turns - jnp.floor(turns + 0.5)
            z = x * x
            cos = COS_C[6]
            for v in COS_C[5::-1]:
                cos = cos * z + v
            sin = SIN_C[6]
            for v in SIN_C[5::-1]:
                sin = sin * z + v
            o_ref[0, here, k * 128 : (k + 1) * 128] = (cos * w).astype(jnp.bfloat16)
            o_ref[0, here, (k + 1) * 128 : (k + 2) * 128] = (sin * (x * (w * w))).astype(jnp.bfloat16)

        @pl.when(jnp.logical_not(any_entry))
        def _():
            o_ref[0, here, k * 128 : (k + 2) * 128] = jnp.zeros((TILE_ROWS, 256), jnp.bfloat16)

    def tile(t, _):
        start = pl.multiple_of(t * TILE_ROWS, TILE_ROWS)
        other = DET - 1 - t
        edge = jnp.where(t == 0, DET // 2, DET - t)
        i = start + row
        freq_y = i.astype(f32) * FREQ_STEP
        freq_n = jnp.where(i == 0, -HALF * FREQ_STEP, -freq_y)

        def load(k, t):
            return flags_ref[k * BPD * DET + b * DET + t]

        def direct(t):
            return load(0, t), jnp.full((1, 128), load(0, t), jnp.int32).astype(f32)

        def mirror(t):
            w, w_extra = load(1, t), load(2, t)
            return jnp.abs(w) + jnp.abs(w_extra), jnp.where(col == 0, w_extra, w).astype(f32)

        for k, weights, freq_x in ((0, direct, freq_direct), (2, mirror, freq_mirror)):
            any_here, w_here = weights(t)
            put(k, start, any_here != 0, w_here, freq_x, freq_y)
            any_other, w_other = weights(other)
            any_edge, w_edge = weights(edge)
            w = jnp.where(row == 0, w_edge, w_other)
            put(k + 4, start, jnp.abs(any_other) + jnp.abs(any_edge) != 0, w, freq_x, freq_n)
        return 0

    lax.fori_loop(0, HALF // TILE_ROWS, tile, 0)


def column_kernel(meta_ref, r_ref, phase_hbm, pick_hbm, table_ref, o_ref, *scratch):
    pq_ref, acc_ref, out_ref, phase_ref, pick_ref, sems = scratch
    f32 = jnp.float32
    bf16 = jnp.bfloat16
    copies = [pltpu.make_async_copy(phase_hbm.at[b], phase_ref.at[b], sems.at[b]) for b in range(BPD)]
    copies.append(pltpu.make_async_copy(pick_hbm, pick_ref, sems.at[BPD]))
    for copy in copies:
        copy.start()
    lane = lax.broadcasted_iota(jnp.int32, (1, 128), 1)
    special = meta_ref[1] * COLS + lane % COLS == 0
    keep = jnp.where(special, 0.0, 1.0)

    def products(b):
        left = table_ref[HALF : 2 * HALF + LEFT]
        right = r_ref[:, b * 256 : (b + 1) * 256]
        lanes = slice(b % GROUP * 256, b % GROUP * 256 + 256)
        pq_ref[0, :, lanes] = jnp.dot(left, right, preferred_element_type=f32)

    def lunes(g):
        for q in range(0, HALF, STEP):
            here = slice(q, q + STEP)
            if g == 0:
                sums = [0.0] * 8
            else:
                sums = [acc_ref[here, k * 128 : (k + 1) * 128] for k in range(8)]
            for i in range(GROUP):
                re = slice(i * 256, i * 256 + 128)
                im = slice(i * 256 + 128, i * 256 + 256)
                p1 = pq_ref[0, HALF + q : HALF + q + STEP, re]
                p3 = pq_ref[0, HALF + q : HALF + q + STEP, im]
                p2 = pq_ref[0, here, re]
                p4 = pq_ref[0, here, im]
                phase = [phase_ref[g * GROUP + i, here, k * 128 : (k + 1) * 128].astype(f32) for k in range(8)]
                k3 = keep * p3
                k4 = keep * p4
                n1, n3, nk3 = p1, p3, k3
                if q == 0:
                    first = lax.broadcasted_iota(jnp.int32, (STEP, 128), 0) == 0
                    n1 = jnp.where(first, pq_ref[0, 2 * HALF : 2 * HALF + 1, re], p1)
                    n3 = jnp.where(first, pq_ref[0, 2 * HALF : 2 * HALF + 1, im], p3)
                    nk3 = keep * n3
                pairs = (
                    (p1 + k4, k3 - p2),
                    (jnp.where(special, p3, p1 - k4), -jnp.where(special, p4, k3 + p2)),
                    (n1 - k4, nk3 + p2),
                    (jnp.where(special, n3, n1 + k4), jnp.where(special, p4, p2 - nk3)),
                )
                for j, (g_re, g_im) in enumerate(pairs):
                    cos, sin = phase[2 * j], phase[2 * j + 1]
                    k = (j // 2) * 4 + j % 2
                    sums[k] += g_re * cos - g_im * sin
                    sums[k + 2] += g_re * sin + g_im * cos
            for k in range(8):
                acc_ref[here, k * 128 : (k + 1) * 128] = sums[k]

    for b in range(GROUP):
        products(b)
    for copy in copies[:GROUP]:
        copy.wait()
    for g in range(BPD // GROUP):
        for copy in copies[(g + 1) * GROUP : (g + 2) * GROUP]:
            copy.wait()
        lunes(g)
        if g + 1 < BPD // GROUP:
            for i in range(GROUP):
                products((g + 1) * GROUP + i)

    plain = acc_ref[:, :N]
    negated = acc_ref[:, N:]
    inner = jnp.where(lax.broadcasted_iota(jnp.int32, (HALF, N), 0) == 0, 0.0, negated)
    even_part = jnp.concatenate([plain + inner, negated[:8]], axis=0).astype(bf16)
    odd_part = (plain - inner).astype(bf16)
    even_part = jnp.dot(even_part, pick_ref[:, :128], preferred_element_type=f32)
    odd_part = jnp.dot(odd_part, pick_ref[:, 128:], preferred_element_type=f32)
    nyquist = even_part[HALF : HALF + 1]
    first = lane < 64

    def split(v):
        high = v.astype(bf16).astype(f32)
        return jnp.where(first, high, v - high).astype(bf16)

    by_sin = jnp.dot(table_ref[:N, :HALF], split(odd_part), preferred_element_type=f32)
    by_cos = jnp.dot(table_ref[N:, :HALF], split(even_part[:HALF]), preferred_element_type=f32)
    out_ref[:HALF] = by_cos[:HALF] + by_sin[HALF:]
    out_ref[HALF:] = by_cos[HALF:] + by_sin[:HALF]
    even = out_ref[pl.ds(0, N // 2, stride=2), :]
    odd = out_ref[pl.ds(1, N // 2, stride=2), :]
    out = jnp.where(first, even, odd) + pltpu.roll(jnp.where(first, odd, even), 64, 1)
    o_ref[...] = (out + jnp.where(first, nyquist, -nyquist)).astype(bf16)


def last_kernel(y_ref, table_ref, o_ref):
    f32 = jnp.float32
    bf16 = jnp.bfloat16
    y = y_ref[0:32, :].astype(f32)
    for d in range(1, DET):
        y = y + y_ref[32 * d : 32 * (d + 1), :].astype(f32)
    group = lax.broadcasted_iota(jnp.int32, (8, 128), 1) // 32
    own = lax.broadcasted_iota(jnp.int32, (8, 128), 0) // 2
    tiles = [[] for _ in range(4)]
    for u in range(4):
        rows = y[8 * u : 8 * (u + 1), :]
        turned = [rows] + [pltpu.roll(rows, 32 * k, 1) for k in range(1, 4)]
        for q in range(4):
            tile = jnp.zeros((8, 128), f32)
            for v in range(4):
                tile = jnp.where((own == v) & (group == v), turned[(v - q) % 4], tile)
            tiles[q].append(tile)
    lhs = jnp.concatenate([jnp.concatenate(tiles[q], axis=1) for q in range(4)], axis=0)
    high = lhs.astype(bf16)
    low = (lhs - high.astype(f32)).astype(bf16)
    both = jnp.concatenate([high, low], axis=0)
    out = jnp.dot(both, table_ref[...], preferred_element_type=f32)
    out = out[:32] + out[32:]
    for par in range(2):
        re = out[16 * par : 16 * par + 8]
        im = out[16 * par + 8 : 16 * par + 16]
        image_re = re[:, :N] - im[:, N:]
        image_im = re[:, N:] + im[:, :N]
        for k, image in enumerate((image_re, image_im)):
            image = image[0:4] + image[4:8]
            image = (image[0:2] + image[2:4]) * SCALE
            for h in range(2):
                o_ref[k, 2 * h + par : 2 * h + par + 1, :] = image[h : h + 1]


def shards(intensity, aberrations, lune_blocks, lune_weight):
    det = lax.axis_index("det").astype(jnp.int32)
    scan = lax.axis_index("scan").astype(jnp.int32)
    row_table, col_table, last_table = (jnp.asarray(v) for v in constants())
    bf16 = jnp.bfloat16
    f32 = jnp.float32

    half = scan // 2
    extra = jnp.where(scan % 2 == 0, jnp.where(scan == 0, 8, 16 - half), 15 - half)
    columns = jnp.stack([half, 15 - half, extra])
    blocks = jnp.take(lune_blocks, columns, axis=1)
    weights = jnp.take(lune_weight, columns, axis=1)
    own = det * BPD + jnp.arange(BPD, dtype=jnp.int32)
    hits = blocks[..., None] == own
    flags = jnp.sum(jnp.where(hits, weights[..., None], 0), axis=2)
    flags = flags.transpose(1, 2, 0).reshape(-1)
    meta = jnp.stack([det, scan])

    smem = pl.BlockSpec(memory_space=pltpu.SMEM)
    vmem = pl.BlockSpec(memory_space=pltpu.VMEM)
    hbm = pl.BlockSpec(memory_space=pl.ANY)

    def in_hbm(v):
        return pltpu.with_memory_space_constraint(v, pltpu.HBM)

    def on_chip(v):
        return pltpu.with_memory_space_constraint(v, pltpu.VMEM)

    rows = pl.pallas_call(
        row_kernel,
        in_specs=[hbm, hbm],
        out_specs=hbm,
        out_shape=pltpu.HBM((SCAN, ROWS, BPD * 256), bf16),
        scratch_shapes=[
            pltpu.VMEM((BPD * BLK, ROWS, N), bf16),
            pltpu.VMEM((N, N), bf16),
            pltpu.VMEM((BLK * ROWS, N), f32),
            pltpu.VMEM((SCAN, ROWS, BPD * 256), bf16),
            pltpu.SemaphoreType.DMA((BPD + 1,)),
            pltpu.SemaphoreType.DMA((len(SENDS),)),
        ],
        compiler_params=pltpu.CompilerParams(vmem_limit_bytes=10 << 20),
        name="rows",
    )(in_hbm(intensity), in_hbm(row_table))

    spread = lax.all_to_all(rows.reshape(N, BPD * 256), "scan", 0, 0, tiled=True)

    phases, pick = pl.pallas_call(
        phase_kernel,
        grid=(BPD,),
        in_specs=[smem, smem, smem],
        out_specs=[pl.BlockSpec((1, HALF, 2 * N), lambda b: (b, 0, 0)), pl.BlockSpec((N, 256), lambda b: (0, 0))],
        out_shape=[pltpu.HBM((BPD, HALF, 2 * N), bf16), pltpu.HBM((N, 256), bf16)],
        compiler_params=pltpu.CompilerParams(vmem_limit_bytes=8 << 20),
        name="phases",
    )(meta, flags, aberrations)

    back = pl.pallas_call(
        column_kernel,
        in_specs=[smem, vmem, hbm, hbm, vmem],
        out_specs=vmem,
        out_shape=jax.ShapeDtypeStruct((N // 2, 128), bf16),
        scratch_shapes=[
            pltpu.VMEM((1, HALF + LEFT, GROUP * 256), f32),
            pltpu.VMEM((HALF, 2 * N), f32),
            pltpu.VMEM((N, 128), f32),
            pltpu.VMEM((BPD, HALF, 2 * N), bf16),
            pltpu.VMEM((N, 256), bf16),
            pltpu.SemaphoreType.DMA((BPD + 1,)),
        ],
        compiler_params=pltpu.CompilerParams(vmem_limit_bytes=36 << 20),
        name="columns",
    )(meta, on_chip(spread), in_hbm(phases), in_hbm(pick), on_chip(col_table))

    parts = lax.all_to_all(back.reshape(DET * SCAN, 2, 128), ("det", "scan"), 0, 0, tiled=True)

    return pl.pallas_call(
        last_kernel,
        in_specs=[vmem, vmem],
        out_specs=vmem,
        out_shape=jax.ShapeDtypeStruct((2, 4, N), f32),
        compiler_params=pltpu.CompilerParams(vmem_limit_bytes=6 << 20),
        name="last",
    )(parts.reshape(N // 2, 128), on_chip(last_table))


def solution(mesh):
    return jax.shard_map(
        shards,
        mesh=mesh,
        in_specs=(P("det", "scan", None), P(), P(), P()),
        out_specs=P(None, ("det", "scan"), None),
        check_vma=False,
    )
```

```python
import math

import jax
import jax.numpy as jnp
import numpy as np
from jax import lax
from jax.experimental import pallas as pl
from jax.experimental.pallas import tpu as pltpu
from jax.sharding import PartitionSpec as P

DSIDE = 24
BLK = 8
N = 512
DET = 8
SCAN = 16
BPD = 9
HALF = N // 2
LEFT = HALF + 8
GROUPS = (2, 2, 3, 2)
STEP = 16
WAITS = {0: (1, 2), 2: (3, 4, 5, 6, 7, 8)}
SENDS = (2, 5, 7, 8)
COLS = 16
ROWS = N // SCAN
TILE_ROWS = N // DET
FREQ_STEP = 4.0 / N
PITCH = 2.4 / DSIDE
CENTRE = (DSIDE - 1) / 2.0
QUARTIC = 0.05
SCALE = 1.0 / (N * N * math.sqrt(16 * BLK))


def poly_tables():
    nodes = (0.5 * np.cos((np.arange(64) + 0.5) * np.pi / 64)) ** 2
    z = np.concatenate([nodes, [0.0]])
    x = np.sqrt(z)
    cos_c = np.polynomial.polynomial.polyfit(z, np.cos(2 * np.pi * x), 6)
    ratio = 2 * np.pi * np.sinc(2 * x)
    sin_c = np.polynomial.polynomial.polyfit(z, ratio, 6)
    return [float(v) for v in cos_c], [float(v) for v in sin_c]


COS_C, SIN_C = poly_tables()


def dft_tables():
    n = np.arange(N)
    angle = (n[:, None] * n[None, :] % N) * (2.0 * np.pi / N)
    return np.cos(angle), np.sin(angle)


def constants():
    cos, sin = dft_tables()
    bf16 = jnp.bfloat16
    re_part = cos[:, : N // 2]
    im_part = -sin[:, : N // 2]
    im_part[:, 0] = cos[:, N // 2]
    row_table = np.concatenate([re_part, im_part], axis=1).astype(bf16)
    col_table = np.concatenate([sin[HALF:], sin[:HALF], cos], axis=0).astype(bf16)
    c = np.arange(N // 2).reshape(SCAN, COLS)
    mirrored = N - c
    mirrored[0, 0] = N // 2
    order = np.stack([c, mirrored], axis=1).reshape(-1)
    last_table = np.concatenate([cos[order], sin[order]], axis=1).astype(bf16)
    return row_table, col_table, last_table


def row_kernel(x_hbm, table_hbm, o_hbm, x_ref, table_ref, y_ref, o_ref, sems, out_sems):
    copies = [pltpu.make_async_copy(table_hbm, table_ref, sems.at[BPD])]
    for b in range(BPD):
        here = pl.ds(b * BLK, BLK)
        copies.append(pltpu.make_async_copy(x_hbm.at[here], x_ref.at[here], sems.at[b]))
    for copy in copies:
        copy.start()
    group = lax.broadcasted_iota(jnp.int32, (ROWS, 128), 1) // COLS
    bits = [(group >> k) & 1 == 1 for k in range(3)]

    def transform(b):
        x = x_ref[b * BLK : (b + 1) * BLK].reshape(BLK * ROWS, N)
        y_ref[...] = jnp.dot(x, table_ref[...], preferred_element_type=jnp.float32)

    def exchange(b):
        for part in range(2):
            for half in range(2):
                col = (part * 2 + half) * 128
                a = [y_ref[ROWS * p : ROWS * (p + 1), col : col + 128].astype(jnp.bfloat16) for p in range(BLK)]
                for k in range(3):
                    a = [jnp.where(bits[k], a[(p + (1 << k)) % BLK], a[p]) for p in range(BLK)]
                a = [a[0]] + [pltpu.roll(a[p], COLS * p, 1) for p in range(1, BLK)]
                for k in range(3):
                    a = [jnp.where(bits[k], a[(p + (1 << k)) % BLK], a[p]) for p in range(BLK)]
                col = (b * 2 + part) * 128
                for d in range(BLK):
                    o_ref[half * 8 + d, :, col : col + 128] = a[-d % BLK]

    outs = []
    sent = 0
    copies[0].wait()
    copies[1].wait()
    transform(0)
    for b in range(BPD):
        for i in WAITS.get(b, ()):
            copies[1 + i].wait()
        exchange(b)
        if b + 1 < BPD:
            transform(b + 1)
        if b in SENDS:
            here = pl.ds(sent * 256, (b + 1 - sent) * 256)
            outs.append(pltpu.make_async_copy(o_ref.at[:, :, here], o_hbm.at[:, :, here], out_sems.at[len(outs)]))
            outs[-1].start()
            sent = b + 1
    for copy in outs:
        copy.wait()


def phase_kernel(meta_ref, flags_ref, ab_ref, o_ref, pick_ref):
    f32 = jnp.float32
    b = pl.program_id(0)

    @pl.when(b == 0)
    def _():
        src = lax.broadcasted_iota(jnp.int32, (N, 256), 0)
        dst = lax.broadcasted_iota(jnp.int32, (N, 256), 1)
        for_sin = dst >= 128
        same = (src // 128 % 2 == dst // COLS % 2) & (src % COLS == dst % COLS)
        src_im = src // 256
        dst_im = dst // 32 % 2
        sign = jnp.where(for_sin & (dst_im == 0), -1.0, 1.0)
        match = (src_im == dst_im) != for_sin
        pick_ref[...] = jnp.where(same & match, sign, 0.0).astype(jnp.bfloat16)

    det = meta_ref[0]
    scan = meta_ref[1]
    a0, a1, a2 = ab_ref[0], ab_ref[1], ab_ref[2]
    kappa = QUARTIC * a1
    plus = a0 + a2
    minus = a0 - a2
    lane = lax.broadcasted_iota(jnp.int32, (1, 128), 1)
    pix = lane // COLS
    col = lane % COLS
    column = scan * COLS + col
    special = column == 0
    freq_direct = column.astype(f32) * FREQ_STEP
    freq_mirror = jnp.where(special, -(N // 2) * FREQ_STEP, -freq_direct)
    row = lax.broadcasted_iota(jnp.int32, (TILE_ROWS, 128), 0)
    block = det * BPD + b
    kx = ((lax.rem(block, 3) * BLK + pix).astype(f32) - CENTRE) * PITCH
    ky = (jnp.full((1, 128), lax.div(block, 3), jnp.int32).astype(f32) - CENTRE) * PITCH
    kx2 = kx * kx
    ky2 = ky * ky
    chi_k = plus * kx2 + minus * ky2 + kappa * (kx2 + ky2) * (kx2 + ky2)

    def put(k, start, any_entry, w, freq_x, freq_y):
        here = pl.ds(start, TILE_ROWS)

        @pl.when(any_entry)
        def _():
            ux = kx - w * freq_x
            x2 = ux * ux
            fx = 0.5 * (chi_k - plus * x2 - kappa * x2 * x2)
            dx = -0.5 * minus - kappa * x2
            bx = -0.5 * kappa
            uy = ky - w * freq_y
            y2 = uy * uy
            turns = fx + y2 * (dx + bx * y2)
            x = turns - jnp.floor(turns + 0.5)
            z = x * x
            cos = COS_C[6]
            for v in COS_C[5::-1]:
                cos = cos * z + v
            sin = SIN_C[6]
            for v in SIN_C[5::-1]:
                sin = sin * z + v
            o_ref[0, here, k * 128 : (k + 1) * 128] = (cos * w).astype(jnp.bfloat16)
            o_ref[0, here, (k + 1) * 128 : (k + 2) * 128] = (sin * (x * (w * w))).astype(jnp.bfloat16)

        @pl.when(jnp.logical_not(any_entry))
        def _():
            o_ref[0, here, k * 128 : (k + 2) * 128] = jnp.zeros((TILE_ROWS, 256), jnp.bfloat16)

    def tile(t, _):
        start = pl.multiple_of(t * TILE_ROWS, TILE_ROWS)
        other = DET - 1 - t
        edge = jnp.where(t == 0, DET // 2, DET - t)
        i = start + row
        freq_y = i.astype(f32) * FREQ_STEP
        freq_n = jnp.where(i == 0, -HALF * FREQ_STEP, -freq_y)

        def load(k, t):
            return flags_ref[k * BPD * DET + b * DET + t]

        def direct(t):
            return load(0, t), jnp.full((1, 128), load(0, t), jnp.int32).astype(f32)

        def mirror(t):
            w, w_extra = load(1, t), load(2, t)
            return jnp.abs(w) + jnp.abs(w_extra), jnp.where(col == 0, w_extra, w).astype(f32)

        for k, weights, freq_x in ((0, direct, freq_direct), (2, mirror, freq_mirror)):
            any_here, w_here = weights(t)
            put(k, start, any_here != 0, w_here, freq_x, freq_y)
            any_other, w_other = weights(other)
            any_edge, w_edge = weights(edge)
            w = jnp.where(row == 0, w_edge, w_other)
            put(k + 4, start, jnp.abs(any_other) + jnp.abs(any_edge) != 0, w, freq_x, freq_n)
        return 0

    lax.fori_loop(0, HALF // TILE_ROWS, tile, 0)


def column_kernel(meta_ref, r_ref, phase_hbm, pick_hbm, table_ref, o_ref, *scratch):
    pq_refs, acc_ref, even_ref, odd_ref, out_ref, phase_ref, pick_ref, sems = scratch[:2], *scratch[2:]
    f32 = jnp.float32
    bf16 = jnp.bfloat16
    copies = [pltpu.make_async_copy(phase_hbm.at[b], phase_ref.at[b], sems.at[b]) for b in range(BPD)]
    copies.append(pltpu.make_async_copy(pick_hbm, pick_ref, sems.at[BPD]))
    for copy in copies:
        copy.start()
    lane = lax.broadcasted_iota(jnp.int32, (1, 128), 1)
    special = meta_ref[1] * COLS + lane % COLS == 0
    keep = jnp.where(special, 0.0, 1.0)
    starts = [sum(GROUPS[:g]) for g in range(len(GROUPS))]

    def products(g):
        left = table_ref[HALF : 2 * HALF + LEFT]
        pq_ref = pq_refs[g > 0]
        for i in range(GROUPS[g]):
            b = starts[g] + i
            right = r_ref[:, b * 256 : (b + 1) * 256]
            pq_ref[:, i * 256 : (i + 1) * 256] = jnp.dot(left, right, preferred_element_type=f32)

    def lunes(g):
        pq_ref = pq_refs[g > 0]
        for q in range(0, HALF, STEP):
            here = slice(q, q + STEP)
            first = lax.broadcasted_iota(jnp.int32, (STEP, 128), 0) == 0
            if g == 0:
                sums = [0.0] * 8
            else:
                sums = [acc_ref[here, k * 128 : (k + 1) * 128] for k in range(8)]
            for i in range(GROUPS[g]):
                re = slice(i * 256, i * 256 + 128)
                im = slice(i * 256 + 128, i * 256 + 256)
                p1 = pq_ref[HALF + q : HALF + q + STEP, re]
                p3 = pq_ref[HALF + q : HALF + q + STEP, im]
                p2 = pq_ref[here, re]
                p4 = pq_ref[here, im]
                phase = [phase_ref[starts[g] + i, here, k * 128 : (k + 1) * 128].astype(f32) for k in range(8)]
                k3 = keep * p3
                k4 = keep * p4
                n1, n3, nk3 = p1, p3, k3
                if q == 0:
                    n1 = jnp.where(first, pq_ref[2 * HALF : 2 * HALF + 1, re], p1)
                    n3 = jnp.where(first, pq_ref[2 * HALF : 2 * HALF + 1, im], p3)
                    nk3 = keep * n3
                pairs = (
                    (p1 + k4, k3 - p2),
                    (jnp.where(special, p3, p1 - k4), -jnp.where(special, p4, k3 + p2)),
                    (n1 - k4, nk3 + p2),
                    (jnp.where(special, n3, n1 + k4), jnp.where(special, p4, p2 - nk3)),
                )
                for j, (g_re, g_im) in enumerate(pairs):
                    cos, sin = phase[2 * j], phase[2 * j + 1]
                    k = (j // 2) * 4 + j % 2
                    sums[k] += g_re * cos - g_im * sin
                    sums[k + 2] += g_re * sin + g_im * cos
            for k in range(4):
                lanes = slice(k * 128, (k + 1) * 128)
                if g + 1 < len(GROUPS):
                    acc_ref[here, lanes] = sums[k]
                    acc_ref[here, N + k * 128 : N + (k + 1) * 128] = sums[k + 4]
                    continue
                negated = sums[k + 4]
                if q == 0:
                    even_ref[HALF : HALF + STEP, lanes] = negated.astype(bf16)
                    negated = jnp.where(first, 0.0, negated)
                even_ref[here, lanes] = (sums[k] + negated).astype(bf16)
                odd_ref[here, lanes] = (sums[k] - negated).astype(bf16)

    products(0)
    products(1)
    for g in range(len(GROUPS)):
        for b in range(starts[g], starts[g] + GROUPS[g]):
            copies[b].wait()
        if g + 1 == len(GROUPS):
            copies[BPD].wait()
        lunes(g)
        if 0 < g < len(GROUPS) - 1:
            products(g + 1)

    even_part = jnp.dot(even_ref[...], pick_ref[:, :128], preferred_element_type=f32)
    odd_part = jnp.dot(odd_ref[...], pick_ref[:, 128:], preferred_element_type=f32)
    nyquist = even_part[HALF : HALF + 1]
    left_half = lane < 64

    def split(v):
        high = v.astype(bf16).astype(f32)
        return jnp.where(left_half, high, v - high).astype(bf16)

    by_sin = jnp.dot(table_ref[:N, :HALF], split(odd_part), preferred_element_type=f32)
    by_cos = jnp.dot(table_ref[N:, :HALF], split(even_part[:HALF]), preferred_element_type=f32)
    out_ref[:HALF] = by_cos[:HALF] + by_sin[HALF:]
    out_ref[HALF:] = by_cos[HALF:] + by_sin[:HALF]
    even = out_ref[pl.ds(0, N // 2, stride=2), :]
    odd = out_ref[pl.ds(1, N // 2, stride=2), :]
    out = jnp.where(left_half, even, odd) + pltpu.roll(jnp.where(left_half, odd, even), 64, 1)
    o_ref[...] = (out + jnp.where(left_half, nyquist, -nyquist)).astype(bf16)


def last_kernel(y_ref, table_ref, o_ref):
    f32 = jnp.float32
    bf16 = jnp.bfloat16
    y = y_ref[0:32, :].astype(f32)
    for d in range(1, DET):
        y = y + y_ref[32 * d : 32 * (d + 1), :].astype(f32)
    group = lax.broadcasted_iota(jnp.int32, (8, 128), 1) // 32
    own = lax.broadcasted_iota(jnp.int32, (8, 128), 0) // 2
    tiles = [[] for _ in range(4)]
    for u in range(4):
        rows = y[8 * u : 8 * (u + 1), :]
        turned = [rows] + [pltpu.roll(rows, 32 * k, 1) for k in range(1, 4)]
        for q in range(4):
            tile = jnp.zeros((8, 128), f32)
            for v in range(4):
                tile = jnp.where((own == v) & (group == v), turned[(v - q) % 4], tile)
            tiles[q].append(tile)
    lhs = jnp.concatenate([jnp.concatenate(tiles[q], axis=1) for q in range(4)], axis=0)
    high = lhs.astype(bf16)
    low = (lhs - high.astype(f32)).astype(bf16)
    both = jnp.concatenate([high, low], axis=0)
    out = jnp.dot(both, table_ref[...], preferred_element_type=f32)
    out = out[:32] + out[32:]
    for par in range(2):
        re = out[16 * par : 16 * par + 8]
        im = out[16 * par + 8 : 16 * par + 16]
        image_re = re[:, :N] - im[:, N:]
        image_im = re[:, N:] + im[:, :N]
        for k, image in enumerate((image_re, image_im)):
            image = image[0:4] + image[4:8]
            image = (image[0:2] + image[2:4]) * SCALE
            for h in range(2):
                o_ref[k, 2 * h + par : 2 * h + par + 1, :] = image[h : h + 1]


def shards(intensity, aberrations, lune_blocks, lune_weight):
    det = lax.axis_index("det").astype(jnp.int32)
    scan = lax.axis_index("scan").astype(jnp.int32)
    row_table, col_table, last_table = (jnp.asarray(v) for v in constants())
    bf16 = jnp.bfloat16
    f32 = jnp.float32

    half = scan // 2
    extra = jnp.where(scan % 2 == 0, jnp.where(scan == 0, 8, 16 - half), 15 - half)
    columns = jnp.stack([half, 15 - half, extra])
    blocks = jnp.take(lune_blocks, columns, axis=1)
    weights = jnp.take(lune_weight, columns, axis=1)
    own = det * BPD + jnp.arange(BPD, dtype=jnp.int32)
    hits = blocks[..., None] == own
    flags = jnp.sum(jnp.where(hits, weights[..., None], 0), axis=2)
    flags = flags.transpose(1, 2, 0).reshape(-1)
    meta = jnp.stack([det, scan])

    smem = pl.BlockSpec(memory_space=pltpu.SMEM)
    vmem = pl.BlockSpec(memory_space=pltpu.VMEM)
    hbm = pl.BlockSpec(memory_space=pl.ANY)

    def in_hbm(v):
        return pltpu.with_memory_space_constraint(v, pltpu.HBM)

    def on_chip(v):
        return pltpu.with_memory_space_constraint(v, pltpu.VMEM)

    rows = pl.pallas_call(
        row_kernel,
        in_specs=[hbm, hbm],
        out_specs=hbm,
        out_shape=pltpu.HBM((SCAN, ROWS, BPD * 256), bf16),
        scratch_shapes=[
            pltpu.VMEM((BPD * BLK, ROWS, N), bf16),
            pltpu.VMEM((N, N), bf16),
            pltpu.VMEM((BLK * ROWS, N), f32),
            pltpu.VMEM((SCAN, ROWS, BPD * 256), bf16),
            pltpu.SemaphoreType.DMA((BPD + 1,)),
            pltpu.SemaphoreType.DMA((len(SENDS),)),
        ],
        compiler_params=pltpu.CompilerParams(vmem_limit_bytes=10 << 20),
        name="rows",
    )(in_hbm(intensity), in_hbm(row_table))

    spread = lax.all_to_all(rows.reshape(N, BPD * 256), "scan", 0, 0, tiled=True)

    phases, pick = pl.pallas_call(
        phase_kernel,
        grid=(BPD,),
        in_specs=[smem, smem, smem],
        out_specs=[pl.BlockSpec((1, HALF, 2 * N), lambda b: (b, 0, 0)), pl.BlockSpec((N, 256), lambda b: (0, 0))],
        out_shape=[pltpu.HBM((BPD, HALF, 2 * N), bf16), pltpu.HBM((N, 256), bf16)],
        compiler_params=pltpu.CompilerParams(vmem_limit_bytes=8 << 20),
        name="phases",
    )(meta, flags, aberrations)

    back = pl.pallas_call(
        column_kernel,
        in_specs=[smem, vmem, hbm, hbm, vmem],
        out_specs=vmem,
        out_shape=jax.ShapeDtypeStruct((N // 2, 128), bf16),
        scratch_shapes=[
            pltpu.VMEM((HALF + LEFT, GROUPS[0] * 256), f32),
            pltpu.VMEM((HALF + LEFT, max(GROUPS) * 256), f32),
            pltpu.VMEM((HALF, 2 * N), f32),
            pltpu.VMEM((HALF + STEP, N), bf16),
            pltpu.VMEM((HALF, N), bf16),
            pltpu.VMEM((N, 128), f32),
            pltpu.VMEM((BPD, HALF, 2 * N), bf16),
            pltpu.VMEM((N, 256), bf16),
            pltpu.SemaphoreType.DMA((BPD + 1,)),
        ],
        compiler_params=pltpu.CompilerParams(vmem_limit_bytes=36 << 20),
        name="columns",
    )(meta, on_chip(spread), in_hbm(phases), in_hbm(pick), on_chip(col_table))

    parts = lax.all_to_all(back.reshape(DET * SCAN, 2, 128), ("det", "scan"), 0, 0, tiled=True)

    return pl.pallas_call(
        last_kernel,
        in_specs=[vmem, vmem],
        out_specs=vmem,
        out_shape=jax.ShapeDtypeStruct((2, 4, N), f32),
        compiler_params=pltpu.CompilerParams(vmem_limit_bytes=6 << 20),
        name="last",
    )(parts.reshape(N // 2, 128), on_chip(last_table))


def solution(mesh):
    return jax.shard_map(
        shards,
        mesh=mesh,
        in_specs=(P("det", "scan", None), P(), P(), P()),
        out_specs=P(None, ("det", "scan"), None),
        check_vma=False,
    )
```

```python
import math

import jax
import jax.numpy as jnp
import numpy as np
from jax import lax
from jax.experimental import pallas as pl
from jax.experimental.pallas import tpu as pltpu
from jax.sharding import PartitionSpec as P

DSIDE = 24
BLK = 8
N = 512
DET = 8
SCAN = 16
BPD = 9
HALF = N // 2
LEFT = HALF + 8
PIECE = 32
STEP = 8
WAITS = {0: (1, 2), 2: (3, 4, 5, 6, 7, 8)}
SENDS = (2, 5, 7, 8)
COLS = 16
ROWS = N // SCAN
TILE_ROWS = N // DET
FREQ_STEP = 4.0 / N
PITCH = 2.4 / DSIDE
CENTRE = (DSIDE - 1) / 2.0
QUARTIC = 0.05
SCALE = 1.0 / (N * N * math.sqrt(16 * BLK))


def poly_tables():
    nodes = (0.5 * np.cos((np.arange(64) + 0.5) * np.pi / 64)) ** 2
    z = np.concatenate([nodes, [0.0]])
    x = np.sqrt(z)
    cos_c = np.polynomial.polynomial.polyfit(z, np.cos(2 * np.pi * x), 6)
    ratio = 2 * np.pi * np.sinc(2 * x)
    sin_c = np.polynomial.polynomial.polyfit(z, ratio, 6)
    return [float(v) for v in cos_c], [float(v) for v in sin_c]


COS_C, SIN_C = poly_tables()


def dft_tables():
    n = np.arange(N)
    angle = (n[:, None] * n[None, :] % N) * (2.0 * np.pi / N)
    return np.cos(angle), np.sin(angle)


def constants():
    cos, sin = dft_tables()
    bf16 = jnp.bfloat16
    re_part = cos[:, : N // 2]
    im_part = -sin[:, : N // 2]
    im_part[:, 0] = cos[:, N // 2]
    row_table = np.concatenate([re_part, im_part], axis=1).astype(bf16)
    col_table = np.concatenate([sin[HALF:], sin[:HALF], cos], axis=0).astype(bf16)
    c = np.arange(N // 2).reshape(SCAN, COLS)
    mirrored = N - c
    mirrored[0, 0] = N // 2
    order = np.stack([c, mirrored], axis=1).reshape(-1)
    last_table = np.concatenate([cos[order], sin[order]], axis=1).astype(bf16)
    return row_table, col_table, last_table


def row_kernel(x_hbm, table_hbm, o_hbm, x_ref, table_ref, y_ref, o_ref, sems, out_sems):
    copies = [pltpu.make_async_copy(table_hbm, table_ref, sems.at[BPD])]
    for b in range(BPD):
        here = pl.ds(b * BLK, BLK)
        copies.append(pltpu.make_async_copy(x_hbm.at[here], x_ref.at[here], sems.at[b]))
    for copy in copies:
        copy.start()
    group = lax.broadcasted_iota(jnp.int32, (ROWS, 128), 1) // COLS
    bits = [(group >> k) & 1 == 1 for k in range(3)]

    def transform(b):
        x = x_ref[b * BLK : (b + 1) * BLK].reshape(BLK * ROWS, N)
        y_ref[...] = jnp.dot(x, table_ref[...], preferred_element_type=jnp.float32)

    def exchange(b):
        for part in range(2):
            for half in range(2):
                col = (part * 2 + half) * 128
                a = [y_ref[ROWS * p : ROWS * (p + 1), col : col + 128].astype(jnp.bfloat16) for p in range(BLK)]
                for k in range(3):
                    a = [jnp.where(bits[k], a[(p + (1 << k)) % BLK], a[p]) for p in range(BLK)]
                a = [a[0]] + [pltpu.roll(a[p], COLS * p, 1) for p in range(1, BLK)]
                for k in range(3):
                    a = [jnp.where(bits[k], a[(p + (1 << k)) % BLK], a[p]) for p in range(BLK)]
                col = (b * 2 + part) * 128
                for d in range(BLK):
                    o_ref[half * 8 + d, :, col : col + 128] = a[-d % BLK]

    outs = []
    sent = 0
    copies[0].wait()
    copies[1].wait()
    transform(0)
    for b in range(BPD):
        for i in WAITS.get(b, ()):
            copies[1 + i].wait()
        exchange(b)
        if b + 1 < BPD:
            transform(b + 1)
        if b in SENDS:
            here = pl.ds(sent * 256, (b + 1 - sent) * 256)
            outs.append(pltpu.make_async_copy(o_ref.at[:, :, here], o_hbm.at[:, :, here], out_sems.at[len(outs)]))
            outs[-1].start()
            sent = b + 1
    for copy in outs:
        copy.wait()


def phase_kernel(meta_ref, flags_ref, ab_ref, o_ref, pick_ref):
    f32 = jnp.float32
    b = pl.program_id(0)

    @pl.when(b == 0)
    def _():
        src = lax.broadcasted_iota(jnp.int32, (N, 256), 0)
        dst = lax.broadcasted_iota(jnp.int32, (N, 256), 1)
        for_sin = dst >= 128
        same = (src // 128 % 2 == dst // COLS % 2) & (src % COLS == dst % COLS)
        src_im = src // 256
        dst_im = dst // 32 % 2
        sign = jnp.where(for_sin & (dst_im == 0), -1.0, 1.0)
        match = (src_im == dst_im) != for_sin
        pick_ref[...] = jnp.where(same & match, sign, 0.0).astype(jnp.bfloat16)

    det = meta_ref[0]
    scan = meta_ref[1]
    a0, a1, a2 = ab_ref[0], ab_ref[1], ab_ref[2]
    kappa = QUARTIC * a1
    plus = a0 + a2
    minus = a0 - a2
    lane = lax.broadcasted_iota(jnp.int32, (1, 128), 1)
    pix = lane // COLS
    col = lane % COLS
    column = scan * COLS + col
    special = column == 0
    freq_direct = column.astype(f32) * FREQ_STEP
    freq_mirror = jnp.where(special, -(N // 2) * FREQ_STEP, -freq_direct)
    row = lax.broadcasted_iota(jnp.int32, (TILE_ROWS, 128), 0)
    block = det * BPD + b
    kx = ((lax.rem(block, 3) * BLK + pix).astype(f32) - CENTRE) * PITCH
    ky = (jnp.full((1, 128), lax.div(block, 3), jnp.int32).astype(f32) - CENTRE) * PITCH
    kx2 = kx * kx
    ky2 = ky * ky
    chi_k = plus * kx2 + minus * ky2 + kappa * (kx2 + ky2) * (kx2 + ky2)

    def put(k, start, any_entry, w, freq_x, freq_y):
        here = pl.ds(start, TILE_ROWS)

        @pl.when(any_entry)
        def _():
            ux = kx - w * freq_x
            x2 = ux * ux
            fx = 0.5 * (chi_k - plus * x2 - kappa * x2 * x2)
            dx = -0.5 * minus - kappa * x2
            bx = -0.5 * kappa
            uy = ky - w * freq_y
            y2 = uy * uy
            turns = fx + y2 * (dx + bx * y2)
            x = turns - jnp.floor(turns + 0.5)
            z = x * x
            cos = COS_C[6]
            for v in COS_C[5::-1]:
                cos = cos * z + v
            sin = SIN_C[6]
            for v in SIN_C[5::-1]:
                sin = sin * z + v
            o_ref[0, here, k * 128 : (k + 1) * 128] = (cos * w).astype(jnp.bfloat16)
            o_ref[0, here, (k + 1) * 128 : (k + 2) * 128] = (sin * (x * (w * w))).astype(jnp.bfloat16)

        @pl.when(jnp.logical_not(any_entry))
        def _():
            o_ref[0, here, k * 128 : (k + 2) * 128] = jnp.zeros((TILE_ROWS, 256), jnp.bfloat16)

    def tile(t, _):
        start = pl.multiple_of(t * TILE_ROWS, TILE_ROWS)
        other = DET - 1 - t
        edge = jnp.where(t == 0, DET // 2, DET - t)
        i = start + row
        freq_y = i.astype(f32) * FREQ_STEP
        freq_n = jnp.where(i == 0, -HALF * FREQ_STEP, -freq_y)

        def load(k, t):
            return flags_ref[k * BPD * DET + b * DET + t]

        def direct(t):
            return load(0, t), jnp.full((1, 128), load(0, t), jnp.int32).astype(f32)

        def mirror(t):
            w, w_extra = load(1, t), load(2, t)
            return jnp.abs(w) + jnp.abs(w_extra), jnp.where(col == 0, w_extra, w).astype(f32)

        for k, weights, freq_x in ((0, direct, freq_direct), (2, mirror, freq_mirror)):
            any_here, w_here = weights(t)
            put(k, start, any_here != 0, w_here, freq_x, freq_y)
            any_other, w_other = weights(other)
            any_edge, w_edge = weights(edge)
            w = jnp.where(row == 0, w_edge, w_other)
            put(k + 4, start, jnp.abs(any_other) + jnp.abs(any_edge) != 0, w, freq_x, freq_n)
        return 0

    lax.fori_loop(0, HALF // TILE_ROWS, tile, 0)


def column_kernel(meta_ref, r_ref, phase_hbm, pick_hbm, table_ref, o_ref, *scratch):
    pq_ref, even_ref, odd_ref, out_ref, phase_ref, pick_ref, sems = scratch
    f32 = jnp.float32
    bf16 = jnp.bfloat16
    copies = []
    for i in range(HALF // PIECE):
        piece = pl.ds(i * PIECE, PIECE)
        copies.append(pltpu.make_async_copy(phase_hbm.at[:, piece], phase_ref.at[:, piece], sems.at[i]))
    copies.append(pltpu.make_async_copy(pick_hbm, pick_ref, sems.at[HALF // PIECE]))
    for copy in copies:
        copy.start()
    lane = lax.broadcasted_iota(jnp.int32, (1, 128), 1)
    special = meta_ref[1] * COLS + lane % COLS == 0
    keep = jnp.where(special, 0.0, 1.0)
    left = table_ref[HALF : 2 * HALF + LEFT]
    for b in range(BPD):
        lanes = slice(b * 256, (b + 1) * 256)
        pq_ref[:, lanes] = jnp.dot(left, r_ref[:, lanes], preferred_element_type=f32)

    def lunes(begin):
        for q in range(begin, begin + PIECE, STEP):
            here = slice(q, q + STEP)
            first = lax.broadcasted_iota(jnp.int32, (STEP, 128), 0) == 0
            sums = [0.0] * 8
            for i in range(BPD):
                re = slice(i * 256, i * 256 + 128)
                im = slice(i * 256 + 128, i * 256 + 256)
                p1 = pq_ref[HALF + q : HALF + q + STEP, re]
                p3 = pq_ref[HALF + q : HALF + q + STEP, im]
                p2 = pq_ref[here, re]
                p4 = pq_ref[here, im]
                phase = [phase_ref[i, here, k * 128 : (k + 1) * 128].astype(f32) for k in range(8)]
                k3 = keep * p3
                k4 = keep * p4
                n1, n3, nk3 = p1, p3, k3
                if q == 0:
                    n1 = jnp.where(first, pq_ref[2 * HALF : 2 * HALF + 1, re], p1)
                    n3 = jnp.where(first, pq_ref[2 * HALF : 2 * HALF + 1, im], p3)
                    nk3 = keep * n3
                pairs = (
                    (p1 + k4, k3 - p2),
                    (jnp.where(special, p3, p1 - k4), -jnp.where(special, p4, k3 + p2)),
                    (n1 - k4, nk3 + p2),
                    (jnp.where(special, n3, n1 + k4), jnp.where(special, p4, p2 - nk3)),
                )
                for j, (g_re, g_im) in enumerate(pairs):
                    cos, sin = phase[2 * j], phase[2 * j + 1]
                    k = (j // 2) * 4 + j % 2
                    sums[k] += g_re * cos - g_im * sin
                    sums[k + 2] += g_re * sin + g_im * cos
            for k in range(4):
                lanes = slice(k * 128, (k + 1) * 128)
                negated = sums[k + 4]
                if q == 0:
                    even_ref[HALF : HALF + STEP, lanes] = negated.astype(bf16)
                    negated = jnp.where(first, 0.0, negated)
                even_ref[here, lanes] = (sums[k] + negated).astype(bf16)
                odd_ref[here, lanes] = (sums[k] - negated).astype(bf16)

    for i in range(HALF // PIECE):
        copies[i].wait()
        lunes(i * PIECE)

    copies[-1].wait()
    even_part = jnp.dot(even_ref[...], pick_ref[:, :128], preferred_element_type=f32)
    odd_part = jnp.dot(odd_ref[...], pick_ref[:, 128:], preferred_element_type=f32)
    nyquist = even_part[HALF : HALF + 1]
    left_half = lane < 64

    def split(v):
        high = v.astype(bf16).astype(f32)
        return jnp.where(left_half, high, v - high).astype(bf16)

    by_sin = jnp.dot(table_ref[:N, :HALF], split(odd_part), preferred_element_type=f32)
    by_cos = jnp.dot(table_ref[N:, :HALF], split(even_part[:HALF]), preferred_element_type=f32)
    out_ref[:HALF] = by_cos[:HALF] + by_sin[HALF:]
    out_ref[HALF:] = by_cos[HALF:] + by_sin[:HALF]
    even = out_ref[pl.ds(0, N // 2, stride=2), :]
    odd = out_ref[pl.ds(1, N // 2, stride=2), :]
    out = jnp.where(left_half, even, odd) + pltpu.roll(jnp.where(left_half, odd, even), 64, 1)
    o_ref[...] = (out + jnp.where(left_half, nyquist, -nyquist)).astype(bf16)


def last_kernel(y_ref, table_ref, o_ref):
    f32 = jnp.float32
    bf16 = jnp.bfloat16
    y = y_ref[0:32, :].astype(f32)
    for d in range(1, DET):
        y = y + y_ref[32 * d : 32 * (d + 1), :].astype(f32)
    group = lax.broadcasted_iota(jnp.int32, (8, 128), 1) // 32
    own = lax.broadcasted_iota(jnp.int32, (8, 128), 0) // 2
    tiles = [[] for _ in range(4)]
    for u in range(4):
        rows = y[8 * u : 8 * (u + 1), :]
        turned = [rows] + [pltpu.roll(rows, 32 * k, 1) for k in range(1, 4)]
        for q in range(4):
            tile = jnp.zeros((8, 128), f32)
            for v in range(4):
                tile = jnp.where((own == v) & (group == v), turned[(v - q) % 4], tile)
            tiles[q].append(tile)
    lhs = jnp.concatenate([jnp.concatenate(tiles[q], axis=1) for q in range(4)], axis=0)
    high = lhs.astype(bf16)
    low = (lhs - high.astype(f32)).astype(bf16)
    both = jnp.concatenate([high, low], axis=0)
    out = jnp.dot(both, table_ref[...], preferred_element_type=f32)
    out = out[:32] + out[32:]
    for par in range(2):
        re = out[16 * par : 16 * par + 8]
        im = out[16 * par + 8 : 16 * par + 16]
        image_re = re[:, :N] - im[:, N:]
        image_im = re[:, N:] + im[:, :N]
        for k, image in enumerate((image_re, image_im)):
            image = image[0:4] + image[4:8]
            image = (image[0:2] + image[2:4]) * SCALE
            for h in range(2):
                o_ref[k, 2 * h + par : 2 * h + par + 1, :] = image[h : h + 1]


def shards(intensity, aberrations, lune_blocks, lune_weight):
    det = lax.axis_index("det").astype(jnp.int32)
    scan = lax.axis_index("scan").astype(jnp.int32)
    row_table, col_table, last_table = (jnp.asarray(v) for v in constants())
    bf16 = jnp.bfloat16
    f32 = jnp.float32

    half = scan // 2
    extra = jnp.where(scan % 2 == 0, jnp.where(scan == 0, 8, 16 - half), 15 - half)
    columns = jnp.stack([half, 15 - half, extra])
    blocks = jnp.take(lune_blocks, columns, axis=1)
    weights = jnp.take(lune_weight, columns, axis=1)
    own = det * BPD + jnp.arange(BPD, dtype=jnp.int32)
    hits = blocks[..., None] == own
    flags = jnp.sum(jnp.where(hits, weights[..., None], 0), axis=2)
    flags = flags.transpose(1, 2, 0).reshape(-1)
    meta = jnp.stack([det, scan])

    smem = pl.BlockSpec(memory_space=pltpu.SMEM)
    vmem = pl.BlockSpec(memory_space=pltpu.VMEM)
    hbm = pl.BlockSpec(memory_space=pl.ANY)

    def in_hbm(v):
        return pltpu.with_memory_space_constraint(v, pltpu.HBM)

    def on_chip(v):
        return pltpu.with_memory_space_constraint(v, pltpu.VMEM)

    rows = pl.pallas_call(
        row_kernel,
        in_specs=[hbm, hbm],
        out_specs=hbm,
        out_shape=pltpu.HBM((SCAN, ROWS, BPD * 256), bf16),
        scratch_shapes=[
            pltpu.VMEM((BPD * BLK, ROWS, N), bf16),
            pltpu.VMEM((N, N), bf16),
            pltpu.VMEM((BLK * ROWS, N), f32),
            pltpu.VMEM((SCAN, ROWS, BPD * 256), bf16),
            pltpu.SemaphoreType.DMA((BPD + 1,)),
            pltpu.SemaphoreType.DMA((len(SENDS),)),
        ],
        compiler_params=pltpu.CompilerParams(vmem_limit_bytes=10 << 20),
        name="rows",
    )(in_hbm(intensity), in_hbm(row_table))

    spread = lax.all_to_all(rows.reshape(N, BPD * 256), "scan", 0, 0, tiled=True)

    phases, pick = pl.pallas_call(
        phase_kernel,
        grid=(BPD,),
        in_specs=[smem, smem, smem],
        out_specs=[pl.BlockSpec((1, HALF, 2 * N), lambda b: (b, 0, 0)), pl.BlockSpec((N, 256), lambda b: (0, 0))],
        out_shape=[pltpu.HBM((BPD, HALF, 2 * N), bf16), pltpu.HBM((N, 256), bf16)],
        compiler_params=pltpu.CompilerParams(vmem_limit_bytes=8 << 20),
        name="phases",
    )(meta, flags, aberrations)

    back = pl.pallas_call(
        column_kernel,
        in_specs=[smem, vmem, hbm, hbm, vmem],
        out_specs=vmem,
        out_shape=jax.ShapeDtypeStruct((N // 2, 128), bf16),
        scratch_shapes=[
            pltpu.VMEM((HALF + LEFT, BPD * 256), f32),
            pltpu.VMEM((HALF + STEP, N), bf16),
            pltpu.VMEM((HALF, N), bf16),
            pltpu.VMEM((N, 128), f32),
            pltpu.VMEM((BPD, HALF, 2 * N), bf16),
            pltpu.VMEM((N, 256), bf16),
            pltpu.SemaphoreType.DMA((HALF // PIECE + 1,)),
        ],
        compiler_params=pltpu.CompilerParams(vmem_limit_bytes=36 << 20),
        name="columns",
    )(meta, on_chip(spread), in_hbm(phases), in_hbm(pick), on_chip(col_table))

    parts = lax.all_to_all(back.reshape(DET * SCAN, 2, 128), ("det", "scan"), 0, 0, tiled=True)

    return pl.pallas_call(
        last_kernel,
        in_specs=[vmem, vmem],
        out_specs=vmem,
        out_shape=jax.ShapeDtypeStruct((2, 4, N), f32),
        compiler_params=pltpu.CompilerParams(vmem_limit_bytes=6 << 20),
        name="last",
    )(parts.reshape(N // 2, 128), on_chip(last_table))


def solution(mesh):
    return jax.shard_map(
        shards,
        mesh=mesh,
        in_specs=(P("det", "scan", None), P(), P(), P()),
        out_specs=P(None, ("det", "scan"), None),
        check_vma=False,
    )
```

```python
import math

import jax
import jax.numpy as jnp
import numpy as np
from jax import lax
from jax.experimental import pallas as pl
from jax.experimental.pallas import tpu as pltpu
from jax.sharding import PartitionSpec as P

DSIDE = 24
BLK = 8
N = 512
DET = 8
SCAN = 16
BPD = 9
HALF = N // 2
LEFT = HALF + 8
PIECE = 32
STEP = 8
WAITS = {0: (1, 2), 2: (3, 4, 5, 6, 7, 8)}
SENDS = (2, 5, 7, 8)
COLS = 16
ROWS = N // SCAN
TILE_ROWS = N // DET
FREQ_STEP = 4.0 / N
PITCH = 2.4 / DSIDE
CENTRE = (DSIDE - 1) / 2.0
QUARTIC = 0.05
SCALE = 1.0 / (N * N * math.sqrt(16 * BLK))


def poly_tables():
    nodes = (0.5 * np.cos((np.arange(64) + 0.5) * np.pi / 64)) ** 2
    z = np.concatenate([nodes, [0.0]])
    x = np.sqrt(z)
    cos_c = np.polynomial.polynomial.polyfit(z, np.cos(2 * np.pi * x), 6)
    ratio = 2 * np.pi * np.sinc(2 * x)
    sin_c = np.polynomial.polynomial.polyfit(z, ratio, 6)
    return [float(v) for v in cos_c], [float(v) for v in sin_c]


COS_C, SIN_C = poly_tables()


def dft_tables():
    n = np.arange(N)
    angle = (n[:, None] * n[None, :] % N) * (2.0 * np.pi / N)
    return np.cos(angle), np.sin(angle)


def constants():
    cos, sin = dft_tables()
    bf16 = jnp.bfloat16
    re_part = cos[:, : N // 2]
    im_part = -sin[:, : N // 2]
    im_part[:, 0] = cos[:, N // 2]
    row_table = np.concatenate([re_part, im_part], axis=1).astype(bf16)
    col_table = np.concatenate([sin[HALF:], sin[:HALF], cos], axis=0).astype(bf16)
    c = np.arange(N // 2).reshape(SCAN, COLS)
    mirrored = N - c
    mirrored[0, 0] = N // 2
    order = np.stack([c, mirrored], axis=1).reshape(-1)
    last_table = np.concatenate([cos[order], sin[order]], axis=1).astype(bf16)
    return row_table, col_table, last_table


def row_kernel(x_hbm, table_hbm, o_hbm, x_ref, table_ref, y_ref, o_ref, sems, out_sems):
    copies = [pltpu.make_async_copy(table_hbm, table_ref, sems.at[BPD])]
    for b in range(BPD):
        here = pl.ds(b * BLK, BLK)
        copies.append(pltpu.make_async_copy(x_hbm.at[here], x_ref.at[here], sems.at[b]))
    for copy in copies:
        copy.start()
    group = lax.broadcasted_iota(jnp.int32, (ROWS, 128), 1) // COLS
    bits = [(group >> k) & 1 == 1 for k in range(3)]

    def transform(b):
        x = x_ref[b * BLK : (b + 1) * BLK].reshape(BLK * ROWS, N)
        y_ref[...] = jnp.dot(x, table_ref[...], preferred_element_type=jnp.float32)

    def exchange(b):
        for part in range(2):
            for half in range(2):
                col = (part * 2 + half) * 128
                a = [y_ref[ROWS * p : ROWS * (p + 1), col : col + 128].astype(jnp.bfloat16) for p in range(BLK)]
                for k in range(3):
                    a = [jnp.where(bits[k], a[(p + (1 << k)) % BLK], a[p]) for p in range(BLK)]
                a = [a[0]] + [pltpu.roll(a[p], COLS * p, 1) for p in range(1, BLK)]
                for k in range(3):
                    a = [jnp.where(bits[k], a[(p + (1 << k)) % BLK], a[p]) for p in range(BLK)]
                col = (b * 2 + part) * 128
                for d in range(BLK):
                    o_ref[half * 8 + d, :, col : col + 128] = a[-d % BLK]

    outs = []
    sent = 0
    copies[0].wait()
    copies[1].wait()
    transform(0)
    for b in range(BPD):
        for i in WAITS.get(b, ()):
            copies[1 + i].wait()
        exchange(b)
        if b + 1 < BPD:
            transform(b + 1)
        if b in SENDS:
            here = pl.ds(sent * 256, (b + 1 - sent) * 256)
            outs.append(pltpu.make_async_copy(o_ref.at[:, :, here], o_hbm.at[:, :, here], out_sems.at[len(outs)]))
            outs[-1].start()
            sent = b + 1
    for copy in outs:
        copy.wait()


def phase_kernel(meta_ref, flags_ref, ab_ref, o_ref, pick_ref):
    f32 = jnp.float32
    b = pl.program_id(0)

    @pl.when(b == 0)
    def _():
        src = lax.broadcasted_iota(jnp.int32, (N, 256), 0)
        dst = lax.broadcasted_iota(jnp.int32, (N, 256), 1)
        for_sin = dst >= 128
        same = (src // 128 % 2 == dst // COLS % 2) & (src % COLS == dst % COLS)
        src_im = src // 256
        dst_im = dst // 32 % 2
        sign = jnp.where(for_sin & (dst_im == 0), -1.0, 1.0)
        match = (src_im == dst_im) != for_sin
        pick_ref[...] = jnp.where(same & match, sign, 0.0).astype(jnp.bfloat16)

    det = meta_ref[0]
    scan = meta_ref[1]
    a0, a1, a2 = ab_ref[0], ab_ref[1], ab_ref[2]
    kappa = QUARTIC * a1
    plus = a0 + a2
    minus = a0 - a2
    lane = lax.broadcasted_iota(jnp.int32, (1, 128), 1)
    pix = lane // COLS
    col = lane % COLS
    column = scan * COLS + col
    special = column == 0
    freq_direct = column.astype(f32) * FREQ_STEP
    freq_mirror = jnp.where(special, -(N // 2) * FREQ_STEP, -freq_direct)
    row = lax.broadcasted_iota(jnp.int32, (TILE_ROWS, 128), 0)
    block = det * BPD + b
    kx = ((lax.rem(block, 3) * BLK + pix).astype(f32) - CENTRE) * PITCH
    ky = (jnp.full((1, 128), lax.div(block, 3), jnp.int32).astype(f32) - CENTRE) * PITCH
    kx2 = kx * kx
    ky2 = ky * ky
    chi_k = plus * kx2 + minus * ky2 + kappa * (kx2 + ky2) * (kx2 + ky2)

    def put(k, start, any_entry, w, freq_x, freq_y):
        here = pl.ds(start, TILE_ROWS)

        @pl.when(any_entry)
        def _():
            ux = kx - w * freq_x
            x2 = ux * ux
            fx = 0.5 * (chi_k - plus * x2 - kappa * x2 * x2)
            dx = -0.5 * minus - kappa * x2
            bx = -0.5 * kappa
            uy = ky - w * freq_y
            y2 = uy * uy
            turns = fx + y2 * (dx + bx * y2)
            x = turns - jnp.floor(turns + 0.5)
            z = x * x
            cos = COS_C[6]
            for v in COS_C[5::-1]:
                cos = cos * z + v
            sin = SIN_C[6]
            for v in SIN_C[5::-1]:
                sin = sin * z + v
            o_ref[0, here, k * 128 : (k + 1) * 128] = (cos * w).astype(jnp.bfloat16)
            o_ref[0, here, (k + 1) * 128 : (k + 2) * 128] = (sin * (x * (w * w))).astype(jnp.bfloat16)

        @pl.when(jnp.logical_not(any_entry))
        def _():
            o_ref[0, here, k * 128 : (k + 2) * 128] = jnp.zeros((TILE_ROWS, 256), jnp.bfloat16)

    def tile(t, _):
        start = pl.multiple_of(t * TILE_ROWS, TILE_ROWS)
        other = DET - 1 - t
        edge = jnp.where(t == 0, DET // 2, DET - t)
        i = start + row
        freq_y = i.astype(f32) * FREQ_STEP
        freq_n = jnp.where(i == 0, -HALF * FREQ_STEP, -freq_y)

        def load(k, t):
            return flags_ref[k * BPD * DET + b * DET + t]

        def direct(t):
            return load(0, t), jnp.full((1, 128), load(0, t), jnp.int32).astype(f32)

        def mirror(t):
            w, w_extra = load(1, t), load(2, t)
            return jnp.abs(w) + jnp.abs(w_extra), jnp.where(col == 0, w_extra, w).astype(f32)

        for k, weights, freq_x in ((0, direct, freq_direct), (2, mirror, freq_mirror)):
            any_here, w_here = weights(t)
            put(k, start, any_here != 0, w_here, freq_x, freq_y)
            any_other, w_other = weights(other)
            any_edge, w_edge = weights(edge)
            w = jnp.where(row == 0, w_edge, w_other)
            put(k + 4, start, jnp.abs(any_other) + jnp.abs(any_edge) != 0, w, freq_x, freq_n)
        return 0

    lax.fori_loop(0, HALF // TILE_ROWS, tile, 0)


def column_kernel(meta_ref, r_ref, phase_hbm, pick_hbm, table_ref, o_ref, *scratch):
    pq_ref, even_ref, odd_ref, out_ref, phase_ref, pick_ref, sems = scratch
    f32 = jnp.float32
    bf16 = jnp.bfloat16
    copies = []
    for i in range(HALF // PIECE):
        piece = pl.ds(i * PIECE, PIECE)
        copies.append(pltpu.make_async_copy(phase_hbm.at[:, piece], phase_ref.at[:, piece], sems.at[i]))
    copies.append(pltpu.make_async_copy(pick_hbm, pick_ref, sems.at[HALF // PIECE]))
    for copy in copies:
        copy.start()
    lane = lax.broadcasted_iota(jnp.int32, (1, 128), 1)
    special = meta_ref[1] * COLS + lane % COLS == 0
    keep = jnp.where(special, 0.0, 1.0)
    left = table_ref[HALF : 2 * HALF + LEFT]
    for b in range(BPD):
        lanes = slice(b * 256, (b + 1) * 256)
        pq_ref[:, lanes] = jnp.dot(left, r_ref[:, lanes], preferred_element_type=f32)

    def lunes(begin):
        for q in range(begin, begin + PIECE, STEP):
            here = slice(q, q + STEP)
            first = lax.broadcasted_iota(jnp.int32, (STEP, 128), 0) == 0
            sums = [None] * 8
            for i in range(BPD):
                re = slice(i * 256, i * 256 + 128)
                im = slice(i * 256 + 128, i * 256 + 256)
                p1 = pq_ref[HALF + q : HALF + q + STEP, re]
                p3 = pq_ref[HALF + q : HALF + q + STEP, im]
                p2 = pq_ref[here, re]
                p4 = pq_ref[here, im]
                phase = [phase_ref[i, here, k * 128 : (k + 1) * 128].astype(f32) for k in range(8)]
                k3 = keep * p3
                k4 = keep * p4
                n1, n3, nk3 = p1, p3, k3
                if q == 0:
                    n1 = jnp.where(first, pq_ref[2 * HALF : 2 * HALF + 1, re], p1)
                    n3 = jnp.where(first, pq_ref[2 * HALF : 2 * HALF + 1, im], p3)
                    nk3 = keep * n3
                pairs = (
                    (p1 + k4, k3 - p2),
                    (jnp.where(special, p3, p1 - k4), jnp.where(special, p4, k3 + p2)),
                    (n1 - k4, nk3 + p2),
                    (jnp.where(special, n3, n1 + k4), jnp.where(special, p4, p2 - nk3)),
                )
                for j, (g_re, g_im) in enumerate(pairs):
                    cos, sin = phase[2 * j], phase[2 * j + 1]
                    k = (j // 2) * 4 + j % 2
                    if j == 1:
                        terms = (g_re * cos + g_im * sin, g_re * sin - g_im * cos)
                    else:
                        terms = (g_re * cos - g_im * sin, g_re * sin + g_im * cos)
                    for slot, term in zip((k, k + 2), terms):
                        sums[slot] = term if sums[slot] is None else sums[slot] + term
            for k in range(4):
                lanes = slice(k * 128, (k + 1) * 128)
                negated = sums[k + 4]
                if q == 0:
                    even_ref[HALF : HALF + STEP, lanes] = negated.astype(bf16)
                    negated = jnp.where(first, 0.0, negated)
                even_ref[here, lanes] = (sums[k] + negated).astype(bf16)
                odd_ref[here, lanes] = (sums[k] - negated).astype(bf16)

    for i in range(HALF // PIECE):
        copies[i].wait()
        lunes(i * PIECE)

    copies[-1].wait()
    even_part = jnp.dot(even_ref[...], pick_ref[:, :128], preferred_element_type=f32)
    odd_part = jnp.dot(odd_ref[...], pick_ref[:, 128:], preferred_element_type=f32)
    nyquist = even_part[HALF : HALF + 1]
    left_half = lane < 64

    def split(v):
        high = v.astype(bf16).astype(f32)
        return jnp.where(left_half, high, v - high).astype(bf16)

    by_sin = jnp.dot(table_ref[:N, :HALF], split(odd_part), preferred_element_type=f32)
    by_cos = jnp.dot(table_ref[N:, :HALF], split(even_part[:HALF]), preferred_element_type=f32)
    out_ref[:HALF] = by_cos[:HALF] + by_sin[HALF:]
    out_ref[HALF:] = by_cos[HALF:] + by_sin[:HALF]
    even = out_ref[pl.ds(0, N // 2, stride=2), :]
    odd = out_ref[pl.ds(1, N // 2, stride=2), :]
    out = jnp.where(left_half, even, odd) + pltpu.roll(jnp.where(left_half, odd, even), 64, 1)
    o_ref[...] = (out + jnp.where(left_half, nyquist, -nyquist)).astype(bf16)


def last_kernel(y_ref, table_ref, o_ref):
    f32 = jnp.float32
    bf16 = jnp.bfloat16
    y = y_ref[0:32, :].astype(f32)
    for d in range(1, DET):
        y = y + y_ref[32 * d : 32 * (d + 1), :].astype(f32)
    group = lax.broadcasted_iota(jnp.int32, (8, 128), 1) // 32
    own = lax.broadcasted_iota(jnp.int32, (8, 128), 0) // 2
    tiles = [[] for _ in range(4)]
    for u in range(4):
        rows = y[8 * u : 8 * (u + 1), :]
        turned = [rows] + [pltpu.roll(rows, 32 * k, 1) for k in range(1, 4)]
        for q in range(4):
            tile = jnp.zeros((8, 128), f32)
            for v in range(4):
                tile = jnp.where((own == v) & (group == v), turned[(v - q) % 4], tile)
            tiles[q].append(tile)
    lhs = jnp.concatenate([jnp.concatenate(tiles[q], axis=1) for q in range(4)], axis=0)
    high = lhs.astype(bf16)
    low = (lhs - high.astype(f32)).astype(bf16)
    both = jnp.concatenate([high, low], axis=0)
    out = jnp.dot(both, table_ref[...], preferred_element_type=f32)
    out = out[:32] + out[32:]
    for par in range(2):
        re = out[16 * par : 16 * par + 8]
        im = out[16 * par + 8 : 16 * par + 16]
        image_re = re[:, :N] - im[:, N:]
        image_im = re[:, N:] + im[:, :N]
        for k, image in enumerate((image_re, image_im)):
            image = image[0:4] + image[4:8]
            image = (image[0:2] + image[2:4]) * SCALE
            for h in range(2):
                o_ref[k, 2 * h + par : 2 * h + par + 1, :] = image[h : h + 1]


def shards(intensity, aberrations, lune_blocks, lune_weight):
    det = lax.axis_index("det").astype(jnp.int32)
    scan = lax.axis_index("scan").astype(jnp.int32)
    row_table, col_table, last_table = (jnp.asarray(v) for v in constants())
    bf16 = jnp.bfloat16
    f32 = jnp.float32

    half = scan // 2
    extra = jnp.where(scan % 2 == 0, jnp.where(scan == 0, 8, 16 - half), 15 - half)
    columns = jnp.stack([half, 15 - half, extra])
    blocks = jnp.take(lune_blocks, columns, axis=1)
    weights = jnp.take(lune_weight, columns, axis=1)
    own = det * BPD + jnp.arange(BPD, dtype=jnp.int32)
    hits = blocks[..., None] == own
    flags = jnp.sum(jnp.where(hits, weights[..., None], 0), axis=2)
    flags = flags.transpose(1, 2, 0).reshape(-1)
    meta = jnp.stack([det, scan])

    smem = pl.BlockSpec(memory_space=pltpu.SMEM)
    vmem = pl.BlockSpec(memory_space=pltpu.VMEM)
    hbm = pl.BlockSpec(memory_space=pl.ANY)

    def in_hbm(v):
        return pltpu.with_memory_space_constraint(v, pltpu.HBM)

    def on_chip(v):
        return pltpu.with_memory_space_constraint(v, pltpu.VMEM)

    rows = pl.pallas_call(
        row_kernel,
        in_specs=[hbm, hbm],
        out_specs=hbm,
        out_shape=pltpu.HBM((SCAN, ROWS, BPD * 256), bf16),
        scratch_shapes=[
            pltpu.VMEM((BPD * BLK, ROWS, N), bf16),
            pltpu.VMEM((N, N), bf16),
            pltpu.VMEM((BLK * ROWS, N), f32),
            pltpu.VMEM((SCAN, ROWS, BPD * 256), bf16),
            pltpu.SemaphoreType.DMA((BPD + 1,)),
            pltpu.SemaphoreType.DMA((len(SENDS),)),
        ],
        compiler_params=pltpu.CompilerParams(vmem_limit_bytes=10 << 20),
        name="rows",
    )(in_hbm(intensity), in_hbm(row_table))

    spread = lax.all_to_all(rows.reshape(N, BPD * 256), "scan", 0, 0, tiled=True)

    phases, pick = pl.pallas_call(
        phase_kernel,
        grid=(BPD,),
        in_specs=[smem, smem, smem],
        out_specs=[pl.BlockSpec((1, HALF, 2 * N), lambda b: (b, 0, 0)), pl.BlockSpec((N, 256), lambda b: (0, 0))],
        out_shape=[pltpu.HBM((BPD, HALF, 2 * N), bf16), pltpu.HBM((N, 256), bf16)],
        compiler_params=pltpu.CompilerParams(vmem_limit_bytes=8 << 20),
        name="phases",
    )(meta, flags, aberrations)

    back = pl.pallas_call(
        column_kernel,
        in_specs=[smem, vmem, hbm, hbm, vmem],
        out_specs=vmem,
        out_shape=jax.ShapeDtypeStruct((N // 2, 128), bf16),
        scratch_shapes=[
            pltpu.VMEM((HALF + LEFT, BPD * 256), f32),
            pltpu.VMEM((HALF + STEP, N), bf16),
            pltpu.VMEM((HALF, N), bf16),
            pltpu.VMEM((N, 128), f32),
            pltpu.VMEM((BPD, HALF, 2 * N), bf16),
            pltpu.VMEM((N, 256), bf16),
            pltpu.SemaphoreType.DMA((HALF // PIECE + 1,)),
        ],
        compiler_params=pltpu.CompilerParams(vmem_limit_bytes=36 << 20),
        name="columns",
    )(meta, on_chip(spread), in_hbm(phases), in_hbm(pick), on_chip(col_table))

    parts = lax.all_to_all(back.reshape(DET * SCAN, 2, 128), ("det", "scan"), 0, 0, tiled=True)

    return pl.pallas_call(
        last_kernel,
        in_specs=[vmem, vmem],
        out_specs=vmem,
        out_shape=jax.ShapeDtypeStruct((2, 4, N), f32),
        compiler_params=pltpu.CompilerParams(vmem_limit_bytes=6 << 20),
        name="last",
    )(parts.reshape(N // 2, 128), on_chip(last_table))


def solution(mesh):
    return jax.shard_map(
        shards,
        mesh=mesh,
        in_specs=(P("det", "scan", None), P(), P(), P()),
        out_specs=P(None, ("det", "scan"), None),
        check_vma=False,
    )
```
